512 devices in a mesh: tile: 32 (over y, x), ir: 16 (over z, core).
Axes of the slice: x: 4, y: 8, z: 8, core: 2. Of those that a mesh axis runs over, the one named last changes fastest.
Arguments:
- samples: bfloat16 [4096, 1024], P(('tile', 'ir')), may hold values from -6 to 6
- ir_spectra: bfloat16 [16, 128, 2, 1024], P(None, 'ir'), may hold values from -0.5 to 0.5
- clip_lengths: int32 [16], replicated, may hold values from 1 to 1024, 4096 in all
- room_ids: int32 [16], replicated, may hold values from 0 to 15
Outputs:
- filtered: float32 [4096, 1024], P(('tile', 'ir'))
The draws below stay inside these ranges and needn't reach their ends.
Inputs may be any that keep to these rules, and one draw needn't show every extreme that they name: `clip_lengths`: the lengths sum to 4096; clips lie end to end in block order.
All inputs are finite; a program needn't handle non-finite values.
Results may differ from the reference program's by a relative error of at most 0.0037.
Values may be sent and summed in bfloat16 or wider, within the bound.
A program may use at most 128 MiB of HBM per device.

```python
import math
import jax
import jax.numpy as jnp
import numpy as np
from jax import lax

B = 1024
P_SIZE = 128
ROOMS = 16
CLIPS = 16
BLK_DEV = 128
TOTAL = 4096
N_TILE = 32


def plant(array, key, low, largest):
    spot = [jax.random.randint(jax.random.fold_in(key, axis), (), 0, length) for axis, length in enumerate(array.shape)]
    main_axis = array.shape.index(max(array.shape))
    neighbour = spot[:main_axis] + [(spot[main_axis] + 1) % array.shape[main_axis]] + spot[main_axis + 1:]
    return array.at[tuple(spot)].set(low).at[tuple(neighbour)].set(largest)


def block_levels(own_key, extent, cuts, low, high):
    level, own = 1.0, jax.random.fold_in(own_key, 6)
    for position, blocks in cuts:
        heights = jnp.exp(jax.random.uniform(jax.random.fold_in(own, position), (blocks,), jnp.float32, low / len(cuts), high / len(cuts)))
        level = level * jnp.repeat(heights, extent[position] // blocks).reshape([-1 if axis == position else 1 for axis in range(len(extent))])
    return level


def length_profile(count, total, limit, skew):
    loads = [(1 << 20) // math.isqrt(rank ** skew) + 1 for rank in range(2, count + 1)]
    rest, given = total - limit - (count - 1), [1] * (count - 1)
    while rest > 0:
        movable = [i for i in range(count - 1) if given[i] < limit]
        pool, left = sum([loads[i] for i in movable]), rest
        for i in movable:
            addition = min(limit - given[i], max(1, left * loads[i] // pool), rest)
            given[i] = given[i] + addition
            rest = rest - addition
    return np.array([limit] + given)


def uneven_parts(key, amount, total, limit, skew):
    if amount == 2:
        one = jax.random.randint(key, (), max(1, total - limit), min(limit, total - 1) + 1)
        return jnp.stack([one, total - one])
    sizes = jnp.asarray(length_profile(amount, total, limit, skew), jnp.int32)
    couples = (amount - 1) // 2
    donor, sink = sizes[1:1 + 2 * couples:2], sizes[2:2 + 2 * couples:2]
    margin = jnp.minimum(donor - 1, limit - sink)
    passed = jax.random.randint(jax.random.fold_in(key, 1), (couples,), 0, 1 << 20) % (margin + 1)
    sizes = sizes.at[1:1 + 2 * couples:2].set(donor - passed).at[2:2 + 2 * couples:2].set(sink + passed)
    return sizes[jax.random.permutation(jax.random.fold_in(key, 2), amount)]


def normal_values(stream_key, extent, scale, most, cuts=(), kind=jnp.bfloat16):
    gain = block_levels(stream_key, extent, cuts, -0.22, 0.18) if cuts else 1.0
    result = jax.random.normal(stream_key, extent, jnp.float32) * scale * gain
    return jnp.minimum(jnp.maximum(result, -most), most).astype(kind)


def setup_inputs(seed: int = 0) -> dict:
    key_list = jax.random.split(jax.random.key(seed), 5)
    return {
        "samples": normal_values(key_list[0], (TOTAL, B), 1.0, 6.0, ((0, 512),)),
        "ir_spectra": normal_values(key_list[1], (ROOMS, P_SIZE, 2, B), P_SIZE ** -0.5, 0.5, ((1, 16),)),
        "clip_lengths": uneven_parts(key_list[2], CLIPS, BLK_DEV * N_TILE, BLK_DEV * N_TILE // 4, 2).astype(jnp.int32),
        "room_ids": plant(jax.random.randint(key_list[3], (CLIPS,), 0, ROOMS), jax.random.fold_in(key_list[3], 1), 0, ROOMS - 1).astype(jnp.int32),
    }


def forward_table(width):
    length = 2 * width
    sample = np.arange(length)
    bins = np.arange(width)
    phase = (sample[:, None] * bins[None, :]) % length
    angle = phase * (2.0 * np.pi / length)
    parity = np.where(sample % 2 == 0, 1.0, -1.0)
    sines = np.where(bins[None, :] == 0, parity[:, None], -np.sin(angle))
    table = np.concatenate([np.cos(angle), sines], axis=1)
    return jnp.asarray(table, dtype=jnp.float32).astype(jnp.bfloat16)


def inverse_table(width):
    length = 2 * width
    bins = np.arange(width)
    outputs = width + np.arange(width)
    phase = (bins[:, None] * outputs[None, :]) % length
    angle = phase * (2.0 * np.pi / length)
    weight = np.where(bins == 0, 1.0, 2.0)[:, None] / length
    parity = np.where(outputs % 2 == 0, 1.0, -1.0)[None, :] / length
    cosines = weight * np.cos(angle)
    sines = np.where(bins[:, None] == 0, parity, -weight * np.sin(angle))
    table = np.concatenate([cosines, sines], axis=0)
    return jnp.asarray(table, dtype=jnp.float32)


def packed_product(spectrum, response, width):
    are, aim = spectrum[:, :width], spectrum[:, width:]
    hre, him = response[:, :width], response[:, width:]
    cross = (jnp.arange(width, dtype=jnp.int32) > 0).astype(jnp.float32)[None, :]
    real = are * hre - cross * aim * him
    imag = cross * (are * him + aim * hre) + (1.0 - cross) * aim * him
    return jnp.concatenate([real, imag], axis=1)


def clip_info(clip_lengths, room_ids, blocks):
    ends = jnp.cumsum(clip_lengths).astype(jnp.int32)
    starts = (ends - clip_lengths).astype(jnp.int32)
    member = (blocks[:, None] >= starts[None, :]) & (blocks[:, None] < ends[None, :])
    begin = jnp.sum(jnp.where(member, starts[None, :], 0), axis=1).astype(jnp.int32)
    room = jnp.sum(jnp.where(member, room_ids[None, :], 0), axis=1).astype(jnp.int32)
    return begin, room


def reference(samples, ir_spectra, clip_lengths, room_ids):
    total, width = samples.shape
    rooms, parts = ir_spectra.shape[0], ir_spectra.shape[1]
    blocks = jnp.arange(total, dtype=jnp.int32)
    begin, room = clip_info(clip_lengths, room_ids, blocks)
    earlier = jnp.concatenate([jnp.zeros((1, width), samples.dtype), samples[:-1]], axis=0)
    earlier = jnp.where((blocks == begin)[:, None], jnp.zeros_like(earlier), earlier)
    frames = jnp.concatenate([earlier, samples], axis=1)
    spectra = jnp.dot(frames, forward_table(width), preferred_element_type=jnp.float32).astype(jnp.bfloat16)
    padded = jnp.concatenate([jnp.zeros((parts - 1, 2 * width), jnp.bfloat16), spectra], axis=0)
    filters = ir_spectra.reshape(rooms, parts, 2 * width)

    def add_partition(index, summed):
        delay = jnp.asarray(index).astype(jnp.int32)
        moved = lax.dynamic_slice_in_dim(padded, (parts - 1 - delay).astype(jnp.int32), total, 0)
        local = lax.dynamic_index_in_dim(filters, delay, 1, keepdims=False)
        chosen = jnp.take(local, room, axis=0)
        live = (blocks - delay) >= begin
        term = packed_product(moved.astype(jnp.float32), chosen.astype(jnp.float32), width)
        return summed + jnp.where(live[:, None], term, jnp.zeros_like(term))

    summed = lax.fori_loop(0, parts, add_partition, jnp.zeros((total, 2 * width), jnp.float32))
    return jnp.dot(summed, inverse_table(width), precision=lax.Precision.HIGHEST, preferred_element_type=jnp.float32)
```

```python
import jax
import jax.numpy as jnp
import numpy as np
from jax import lax
from jax.experimental import pallas as pl
from jax.experimental.pallas import tpu as pltpu
from jax.sharding import PartitionSpec as P

MESH = pl.DeviceIdType.MESH
W = 1024
ROWS = 8
CHIPS = 8
ROOMS = 16
PARTS = 16
OUT = 64
PAIRS = 5
SPAN = PAIRS * 2 * ROWS
SUB = 2 * W // 128
NONE = ROOMS * PARTS


def forward_half(width):
    length = 2 * width
    sample = np.arange(width)
    bins = np.arange(width)
    phase = sample[:, None] * bins[None, :] % length
    angle = phase * (2.0 * np.pi / length)
    parity = np.where(sample % 2 == 0, 1.0, -1.0)
    sines = np.where(bins[None, :] == 0, parity[:, None], -np.sin(angle))
    table = np.concatenate([np.cos(angle), sines], axis=1)
    return jnp.asarray(table, dtype=jnp.float32).astype(jnp.bfloat16)


def inverse_table(width):
    length = 2 * width
    bins = np.arange(width)
    outputs = width + np.arange(width)
    phase = bins[:, None] * outputs[None, :] % length
    angle = phase * (2.0 * np.pi / length)
    weight = np.where(bins == 0, 1.0, 2.0)[:, None] / length
    parity = np.where(outputs % 2 == 0, 1.0, -1.0)[None, :] / length
    cosines = weight * np.cos(angle)
    sines = np.where(bins[:, None] == 0, parity, -weight * np.sin(angle))
    table = np.concatenate([cosines, sines], axis=0)
    return jnp.asarray(table, dtype=jnp.float32).astype(jnp.bfloat16)


def kernel(
    samples,
    ir,
    lengths,
    rooms,
    forward,
    inverse,
    out,
    fwd_v,
    inv_v,
    ir_v,
    filters,
    unpacked,
    held,
    raw,
    spectra,
    summed,
    parts_out,
    arrived,
    choice_v,
    first_v,
    choice,
    first,
    lengths_s,
    rooms_s,
    small_sem,
    table_sem,
    ir_send,
    ir_recv,
    ir_own,
    in_send,
    in_recv,
    out_send,
    out_recv,
):
    tile, ir_at = lax.axis_index("tile"), lax.axis_index("ir")
    tiles = lax.axis_size("tile")
    z, c = ir_at // 2, ir_at % 2
    half = z // 4
    other = 2 * z + 1 - c

    get_lengths = pltpu.make_async_copy(lengths, lengths_s, small_sem.at[0])
    get_rooms = pltpu.make_async_copy(rooms, rooms_s, small_sem.at[1])
    get_lengths.start()
    get_rooms.start()

    barrier = pltpu.get_barrier_semaphore()

    def greet(to):
        pl.semaphore_signal(barrier, inc=1, device_id=to, device_id_type=MESH)

    def source(e, k):
        at = 8 + 4 * c - z - 1 + e
        return (tile + tiles - 1 + at // 8) % tiles, 2 * (at % 8) + k

    own_in = 2 * z + 1 - 4 * c
    for e in range(PAIRS):
        for k in range(2):

            @pl.when(jnp.logical_not((own_in == e) & (c == k)))
            def _(e=e, k=k):
                greet(source(e, k))

    for zs in range(CHIPS):

        @pl.when(jnp.logical_not((z == zs) & (half == c)))
        def _(zs=zs):
            greet((tile, 2 * zs + half))

    greet((tile, other))

    get_own = pltpu.make_async_copy(ir, ir_v.at[c], ir_own)
    get_own.start()
    get_forward = pltpu.make_async_copy(forward, fwd_v, table_sem.at[0])
    get_forward.start()
    get_inverse = pltpu.make_async_copy(inverse, inv_v, table_sem.at[1])
    get_inverse.start()

    own_is_in = ((own_in >= 0) & (own_in < PAIRS)).astype(jnp.int32)
    own_is_out = (half == c).astype(jnp.int32)
    pl.semaphore_wait(barrier, 2 * PAIRS + CHIPS + 1 - own_is_in - own_is_out)

    def target(e, d):
        at = 8 + 4 * d - 1 + e - z
        return (tile + 1 - at // 8) % tiles, 2 * (at % 8) + d

    for e in range(PAIRS):
        for d in range(2):
            itself = (own_in == e) & (c == d)

            @pl.when(itself)
            def _(e=e, d=d):
                pltpu.make_async_copy(samples, held.at[e, c], in_recv.at[e, c]).start()

            @pl.when(jnp.logical_not(itself))
            def _(e=e, d=d):
                pltpu.make_async_remote_copy(
                    src_ref=samples,
                    dst_ref=held.at[e, c],
                    send_sem=in_send.at[e, d],
                    recv_sem=in_recv.at[e, c],
                    device_id=target(e, d),
                    device_id_type=MESH,
                ).start()

    send_ir = pltpu.make_async_remote_copy(
        src_ref=ir,
        dst_ref=ir_v.at[c],
        send_sem=ir_send,
        recv_sem=ir_recv,
        device_id=(tile, other),
        device_id_type=MESH,
    )
    send_ir.start()

    get_lengths.wait()
    get_rooms.wait()
    place = lax.broadcasted_iota(jnp.int32, (8, 128), 0) * 128 + lax.broadcasted_iota(
        jnp.int32, (8, 128), 1
    )
    block = tile * (2 * OUT) + c * OUT + place // PARTS
    delay = z * PARTS + place % PARTS
    row_block = tile * (2 * OUT) + c * OUT - z * PARTS - PARTS + place
    begin = jnp.zeros((8, 128), jnp.int32)
    room = jnp.zeros((8, 128), jnp.int32)
    joined = jnp.ones((8, 128), jnp.float32)
    start = jnp.int32(0)
    for n in range(ROOMS):
        end = start + lengths_s[n]
        member = (block >= start) & (block < end)
        begin = jnp.where(member, start, begin)
        room = jnp.where(member, rooms_s[n], room)
        joined = jnp.where(row_block == start, 0.0, joined)
        start = end
    chosen = jnp.where(block - delay >= begin, room * PARTS + place % PARTS, NONE)
    choice_v[...] = chosen
    first_v[...] = joined
    put_choice = pltpu.make_async_copy(choice_v, choice, small_sem.at[2])
    put_first = pltpu.make_async_copy(first_v, first, small_sem.at[3])
    put_choice.start()
    put_first.start()

    corner = (lax.broadcasted_iota(jnp.int32, (8, 128), 0) == 0) & (
        lax.broadcasted_iota(jnp.int32, (8, 128), 1) == 0
    )
    filters[NONE] = jnp.zeros((3, 8, 128), jnp.float32)

    def unpack(part):
        def step(n, _):
            for p in range(8):
                unpacked[pl.ds(16 * p, 16), :] = ir_v[part, n, p].astype(jnp.float32)
            for p in range(8):
                hre = unpacked[pl.ds(16 * p, 8, stride=2), :]
                him = unpacked[pl.ds(16 * p + 1, 8, stride=2), :]
                at = n * PARTS + part * 8 + p
                filters[at, 0] = hre
                filters[at, 1] = jnp.where(corner, 0.0, him)
                filters[at, 2] = jnp.where(corner, him, hre)
            return 0

        lax.fori_loop(0, ROOMS, step, 0)

    get_own.wait()
    unpack(c)
    send_ir.wait_recv()
    unpack(1 - c)

    put_choice.wait()
    put_first.wait()
    get_forward.wait()
    for e in range(PAIRS):
        for k in range(2):
            pltpu.make_async_copy(samples, held.at[e, k], in_recv.at[e, k]).wait()

    x = held[...].astype(jnp.float32).reshape(SPAN, W).astype(jnp.bfloat16)
    for n in range(2 * W // 256):
        g = jnp.dot(x, fwd_v[:, 256 * n : 256 * n + 256], preferred_element_type=jnp.float32)
        raw[pl.ds(2 * n, SPAN, stride=SUB), :] = g[:, :128]
        raw[pl.ds(2 * n + 1, SPAN, stride=SUB), :] = g[:, 128:]

    sign = 1.0 - 2.0 * (lax.broadcasted_iota(jnp.int32, (SUB, 128), 1) % 2).astype(jnp.float32)
    for r in range(1, SPAN):
        before = raw[pl.ds(SUB * (r - 1), SUB), :]
        own = raw[pl.ds(SUB * r, SUB), :]
        both = first[r // 128, r % 128] * before + sign * own
        spectra[pl.ds(SUB * r, SUB), :] = both.astype(jnp.bfloat16).astype(jnp.float32)

    def eight(b, _):
        res = [jnp.zeros((8, 128), jnp.float32) for _ in range(8)]
        ims = [jnp.zeros((8, 128), jnp.float32) for _ in range(8)]
        for p in range(PARTS):
            for t in range(8):
                at = pl.multiple_of(SUB * (8 * b + t - p + PARTS), 8)
                are = spectra[pl.ds(at, 8), :]
                aim = spectra[pl.ds(at + 8, 8), :]
                h = choice[b, 16 * t + p]
                h0, h1, h2 = filters[h, 0], filters[h, 1], filters[h, 2]
                res[t] = res[t] + (are * h0 - aim * h1)
                ims[t] = ims[t] + (are * h1 + aim * h2)
        for t in range(8):
            to = pl.multiple_of(SUB * (8 * b + t), 8)
            summed[pl.ds(to, 8), :] = res[t]
            summed[pl.ds(to + 8, 8), :] = ims[t]
        return 0

    lax.fori_loop(0, OUT // 8, eight, 0)

    get_inverse.wait()
    y = jnp.concatenate(
        [summed[pl.ds(j, OUT, stride=SUB), :].astype(jnp.bfloat16) for j in range(SUB)], axis=1
    )
    for n in range(W // 256):
        v = jnp.dot(y, inv_v[:, 256 * n : 256 * n + 256], preferred_element_type=jnp.float32)
        for g in range(8):
            parts_out[g, :, 256 * n : 256 * n + 256] = v[8 * g : 8 * g + 8].astype(jnp.bfloat16)

    for g in range(4):
        for k in range(2):
            itself = (z == 4 * c + g) & (c == k)

            @pl.when(itself)
            def _(g=g, k=k):
                pltpu.make_async_copy(
                    parts_out.at[2 * g + k], arrived.at[z], out_recv.at[z]
                ).start()

            @pl.when(jnp.logical_not(itself))
            def _(g=g, k=k):
                pltpu.make_async_remote_copy(
                    src_ref=parts_out.at[2 * g + k],
                    dst_ref=arrived.at[z],
                    send_sem=out_send.at[2 * g + k],
                    recv_sem=out_recv.at[z],
                    device_id=(tile, 2 * (4 * c + g) + k),
                    device_id_type=MESH,
                ).start()

    total = jnp.zeros((ROWS, W), jnp.float32)
    for zs in range(CHIPS):
        pltpu.make_async_copy(parts_out.at[0], arrived.at[zs], out_recv.at[zs]).wait()
        total = total + arrived[zs].astype(jnp.float32)
    out[...] = total

    send_ir.wait_send()
    for e in range(PAIRS):
        for d in range(2):

            @pl.when(jnp.logical_not((own_in == e) & (c == d)))
            def _(e=e, d=d):
                pltpu.make_async_copy(samples, held.at[e, 0], in_send.at[e, d]).wait()

    for g in range(4):
        for k in range(2):

            @pl.when(jnp.logical_not((z == 4 * c + g) & (c == k)))
            def _(g=g, k=k):
                pltpu.make_async_copy(
                    parts_out.at[2 * g + k], arrived.at[0], out_send.at[2 * g + k]
                ).wait()


def on_device(samples, ir_spectra, clip_lengths, room_ids):
    rooms, parts = ir_spectra.shape[0], ir_spectra.shape[1]
    ir = ir_spectra.reshape(rooms, parts, 2, W // 128, 128)
    ir = ir.transpose(0, 1, 3, 2, 4).reshape(rooms, parts, SUB, 128)
    hbm = pl.BlockSpec(memory_space=pl.ANY)
    bf16, f32, dma = jnp.bfloat16, jnp.float32, pltpu.SemaphoreType.DMA
    return pl.pallas_call(
        kernel,
        out_shape=jax.ShapeDtypeStruct((ROWS, W), f32),
        in_specs=[hbm] * 6,
        out_specs=pl.BlockSpec(memory_space=pltpu.VMEM),
        scratch_shapes=[
            pltpu.VMEM((W, 2 * W), bf16),
            pltpu.VMEM((2 * W, W), bf16),
            pltpu.VMEM((2, ROOMS, 8, SUB, 128), bf16),
            pltpu.VMEM((NONE + 1, 3, 8, 128), f32),
            pltpu.VMEM((128, 128), f32),
            pltpu.VMEM((PAIRS, 2, ROWS, W), bf16),
            pltpu.VMEM((SPAN * SUB, 128), f32),
            pltpu.VMEM((SPAN * SUB, 128), f32),
            pltpu.VMEM((OUT * SUB, 128), f32),
            pltpu.VMEM((8, ROWS, W), bf16),
            pltpu.VMEM((CHIPS, ROWS, W), bf16),
            pltpu.VMEM((8, 128), jnp.int32),
            pltpu.VMEM((8, 128), f32),
            pltpu.SMEM((8, 128), jnp.int32),
            pltpu.SMEM((8, 128), f32),
            pltpu.SMEM((ROOMS,), jnp.int32),
            pltpu.SMEM((ROOMS,), jnp.int32),
            dma((4,)),
            dma((2,)),
            dma,
            dma,
            dma,
            dma((PAIRS, 2)),
            dma((PAIRS, 2)),
            dma((8,)),
            dma((CHIPS,)),
        ],
        compiler_params=pltpu.CompilerParams(
            collective_id=0, has_side_effects=True, vmem_limit_bytes=48 * 1024 * 1024
        ),
    )(samples, ir, clip_lengths, room_ids, forward_half(W), inverse_table(W))


def solution(mesh):
    in_specs = (P(("tile", "ir"), None), P(None, "ir", None, None), P(), P())
    out_specs = P(("tile", "ir"), None)
    return jax.shard_map(
        on_device, mesh=mesh, in_specs=in_specs, out_specs=out_specs, check_vma=False
    )
```

```python
import jax
import jax.numpy as jnp
import numpy as np
from jax import lax
from jax.experimental import pallas as pl
from jax.experimental.pallas import tpu as pltpu
from jax.sharding import PartitionSpec as P

MESH = pl.DeviceIdType.MESH
W = 1024
ROWS = 8
CHIPS = 8
ROOMS = 16
PARTS = 16
OUT = 64
PAIRS = 5
SPAN = PAIRS * 2 * ROWS
SUB = 2 * W // 128
NONE = ROOMS * PARTS


def forward_half(width):
    length = 2 * width
    sample = np.arange(width)
    bins = np.arange(width)
    phase = sample[:, None] * bins[None, :] % length
    angle = phase * (2.0 * np.pi / length)
    parity = np.where(sample % 2 == 0, 1.0, -1.0)
    sines = np.where(bins[None, :] == 0, parity[:, None], -np.sin(angle))
    table = np.concatenate([np.cos(angle), sines], axis=1)
    return jnp.asarray(table, dtype=jnp.float32).astype(jnp.bfloat16)


def inverse_table(width):
    length = 2 * width
    bins = np.arange(width)
    outputs = width + np.arange(width)
    phase = bins[:, None] * outputs[None, :] % length
    angle = phase * (2.0 * np.pi / length)
    weight = np.where(bins == 0, 1.0, 2.0)[:, None] / length
    parity = np.where(outputs % 2 == 0, 1.0, -1.0)[None, :] / length
    cosines = weight * np.cos(angle)
    sines = np.where(bins[:, None] == 0, parity, -weight * np.sin(angle))
    table = np.concatenate([cosines, sines], axis=0)
    return jnp.asarray(table, dtype=jnp.float32).astype(jnp.bfloat16)


def kernel(
    samples,
    ir,
    lengths,
    rooms,
    forward,
    inverse,
    out,
    fwd_v,
    inv_v,
    ir_v,
    filters,
    unpacked,
    held,
    raw,
    spectra,
    summed,
    parts_out,
    arrived,
    choice_v,
    first_v,
    choice,
    first,
    lengths_s,
    rooms_s,
    small_sem,
    table_sem,
    ir_send,
    ir_recv,
    ir_own,
    in_send,
    in_recv,
    out_send,
    out_recv,
):
    tile, ir_at = lax.axis_index("tile"), lax.axis_index("ir")
    tiles = lax.axis_size("tile")
    z, c = ir_at // 2, ir_at % 2
    half = z // 4
    other = 2 * z + 1 - c

    get_lengths = pltpu.make_async_copy(lengths, lengths_s, small_sem.at[0])
    get_rooms = pltpu.make_async_copy(rooms, rooms_s, small_sem.at[1])
    get_lengths.start()
    get_rooms.start()

    barrier = pltpu.get_barrier_semaphore()

    def greet(to):
        pl.semaphore_signal(barrier, inc=1, device_id=to, device_id_type=MESH)

    def source(e, k):
        at = 8 + 4 * c - z - 1 + e
        return (tile + tiles - 1 + at // 8) % tiles, 2 * (at % 8) + k

    own_in = 2 * z + 1 - 4 * c
    for e in range(PAIRS):
        for k in range(2):

            @pl.when(jnp.logical_not((own_in == e) & (c == k)))
            def _(e=e, k=k):
                greet(source(e, k))

    for zs in range(CHIPS):

        @pl.when(jnp.logical_not((z == zs) & (half == c)))
        def _(zs=zs):
            greet((tile, 2 * zs + half))

    greet((tile, other))

    get_own = pltpu.make_async_copy(ir, ir_v.at[c], ir_own)
    get_own.start()
    get_forward = pltpu.make_async_copy(forward, fwd_v, table_sem.at[0])
    get_forward.start()
    get_inverse = pltpu.make_async_copy(inverse, inv_v, table_sem.at[1])
    get_inverse.start()

    own_is_in = ((own_in >= 0) & (own_in < PAIRS)).astype(jnp.int32)
    own_is_out = (half == c).astype(jnp.int32)
    pl.semaphore_wait(barrier, 2 * PAIRS + CHIPS + 1 - own_is_in - own_is_out)

    def target(e, d):
        at = 8 + 4 * d - 1 + e - z
        return (tile + 1 - at // 8) % tiles, 2 * (at % 8) + d

    for e in range(PAIRS):
        for d in range(2):
            itself = (own_in == e) & (c == d)

            @pl.when(itself)
            def _(e=e, d=d):
                pltpu.make_async_copy(samples, held.at[e, c], in_recv.at[e, c]).start()

            @pl.when(jnp.logical_not(itself))
            def _(e=e, d=d):
                pltpu.make_async_remote_copy(
                    src_ref=samples,
                    dst_ref=held.at[e, c],
                    send_sem=in_send.at[e, d],
                    recv_sem=in_recv.at[e, c],
                    device_id=target(e, d),
                    device_id_type=MESH,
                ).start()

    send_ir = pltpu.make_async_remote_copy(
        src_ref=ir,
        dst_ref=ir_v.at[c],
        send_sem=ir_send,
        recv_sem=ir_recv,
        device_id=(tile, other),
        device_id_type=MESH,
    )
    send_ir.start()

    get_lengths.wait()
    get_rooms.wait()
    place = lax.broadcasted_iota(jnp.int32, (8, 128), 0) * 128 + lax.broadcasted_iota(
        jnp.int32, (8, 128), 1
    )
    block = tile * (2 * OUT) + c * OUT + place // PARTS
    delay = z * PARTS + place % PARTS
    row_block = tile * (2 * OUT) + c * OUT - z * PARTS - PARTS + place
    begin = jnp.zeros((8, 128), jnp.int32)
    room = jnp.zeros((8, 128), jnp.int32)
    joined = jnp.ones((8, 128), jnp.float32)
    start = jnp.int32(0)
    for n in range(ROOMS):
        end = start + lengths_s[n]
        member = (block >= start) & (block < end)
        begin = jnp.where(member, start, begin)
        room = jnp.where(member, rooms_s[n], room)
        joined = jnp.where(row_block == start, 0.0, joined)
        start = end
    chosen = jnp.where(block - delay >= begin, room * PARTS + place % PARTS, NONE)
    choice_v[...] = chosen
    first_v[...] = joined
    put_choice = pltpu.make_async_copy(choice_v, choice, small_sem.at[2])
    put_first = pltpu.make_async_copy(first_v, first, small_sem.at[3])
    put_choice.start()
    put_first.start()

    corner = (lax.broadcasted_iota(jnp.int32, (8, 128), 0) == 0) & (
        lax.broadcasted_iota(jnp.int32, (8, 128), 1) == 0
    )
    filters[NONE] = jnp.zeros((3, 8, 128), jnp.float32)

    def unpack(part):
        def step(n, _):
            for p in range(8):
                unpacked[pl.ds(16 * p, 16), :] = ir_v[part, n, p].astype(jnp.float32)
            for p in range(8):
                hre = unpacked[pl.ds(16 * p, 8, stride=2), :]
                him = unpacked[pl.ds(16 * p + 1, 8, stride=2), :]
                at = n * PARTS + part * 8 + p
                filters[at, 0] = hre
                filters[at, 1] = jnp.where(corner, 0.0, him)
                filters[at, 2] = jnp.where(corner, him, hre)
            return 0

        lax.fori_loop(0, ROOMS, step, 0)

    get_own.wait()
    unpack(c)
    send_ir.wait_recv()
    unpack(1 - c)

    put_choice.wait()
    put_first.wait()
    get_forward.wait()
    for e in range(PAIRS):
        for k in range(2):
            pltpu.make_async_copy(samples, held.at[e, k], in_recv.at[e, k]).wait()

    x = held[...].astype(jnp.float32).reshape(SPAN, W).astype(jnp.bfloat16)
    for n in range(2 * W // 256):
        g = jnp.dot(x, fwd_v[:, 256 * n : 256 * n + 256], preferred_element_type=jnp.float32)
        raw[pl.ds(2 * n, SPAN, stride=SUB), :] = g[:, :128]
        raw[pl.ds(2 * n + 1, SPAN, stride=SUB), :] = g[:, 128:]

    sign = 1.0 - 2.0 * (lax.broadcasted_iota(jnp.int32, (SUB, 128), 1) % 2).astype(jnp.float32)
    for r in range(1, SPAN):
        before = raw[pl.ds(SUB * (r - 1), SUB), :]
        own = raw[pl.ds(SUB * r, SUB), :]
        both = first[r // 128, r % 128] * before + sign * own
        spectra[pl.ds(SUB * r, SUB), :] = both.astype(jnp.bfloat16).astype(jnp.float32)

    def eight(b, _):
        res = [jnp.zeros((8, 128), jnp.float32) for _ in range(8)]
        ims = [jnp.zeros((8, 128), jnp.float32) for _ in range(8)]
        for p in range(PARTS):
            for t in range(8):
                at = pl.multiple_of(SUB * (8 * b + t - p + PARTS), 8)
                are = spectra[pl.ds(at, 8), :]
                aim = spectra[pl.ds(at + 8, 8), :]
                h = choice[b, 16 * t + p]
                h0, h1, h2 = filters[h, 0], filters[h, 1], filters[h, 2]
                res[t] = res[t] + (are * h0 - aim * h1)
                ims[t] = ims[t] + (are * h1 + aim * h2)
        for t in range(8):
            to = pl.multiple_of(SUB * (8 * b + t), 8)
            summed[pl.ds(to, 8), :] = res[t]
            summed[pl.ds(to + 8, 8), :] = ims[t]
        return 0

    lax.fori_loop(0, OUT // 8, eight, 0)

    get_inverse.wait()
    y = jnp.concatenate(
        [summed[pl.ds(j, OUT, stride=SUB), :].astype(jnp.bfloat16) for j in range(SUB)], axis=1
    )
    for n in range(W // 256):
        v = jnp.dot(y, inv_v[:, 256 * n : 256 * n + 256], preferred_element_type=jnp.float32)
        for g in range(8):
            parts_out[g, :, 256 * n : 256 * n + 256] = v[8 * g : 8 * g + 8].astype(jnp.bfloat16)

    for g in range(4):
        for k in range(2):
            itself = (z == 4 * c + g) & (c == k)

            @pl.when(itself)
            def _(g=g, k=k):
                pltpu.make_async_copy(
                    parts_out.at[2 * g + k], arrived.at[z], out_recv.at[z]
                ).start()

            @pl.when(jnp.logical_not(itself))
            def _(g=g, k=k):
                pltpu.make_async_remote_copy(
                    src_ref=parts_out.at[2 * g + k],
                    dst_ref=arrived.at[z],
                    send_sem=out_send.at[2 * g + k],
                    recv_sem=out_recv.at[z],
                    device_id=(tile, 2 * (4 * c + g) + k),
                    device_id_type=MESH,
                ).start()

    total = jnp.zeros((ROWS, W), jnp.float32)
    for zs in range(CHIPS):
        pltpu.make_async_copy(parts_out.at[0], arrived.at[zs], out_recv.at[zs]).wait()
        total = total + arrived[zs].astype(jnp.float32)
    out[...] = total

    send_ir.wait_send()
    for e in range(PAIRS):
        for d in range(2):

            @pl.when(jnp.logical_not((own_in == e) & (c == d)))
            def _(e=e, d=d):
                pltpu.make_async_copy(samples, held.at[e, 0], in_send.at[e, d]).wait()

    for g in range(4):
        for k in range(2):

            @pl.when(jnp.logical_not((z == 4 * c + g) & (c == k)))
            def _(g=g, k=k):
                pltpu.make_async_copy(
                    parts_out.at[2 * g + k], arrived.at[0], out_send.at[2 * g + k]
                ).wait()


def on_device(samples, ir_spectra, clip_lengths, room_ids):
    rooms, parts = ir_spectra.shape[0], ir_spectra.shape[1]
    ir = ir_spectra.reshape(rooms, parts, 2, W // 128, 128)
    ir = ir.transpose(0, 1, 3, 2, 4).reshape(rooms, parts, SUB, 128)
    hbm = pl.BlockSpec(memory_space=pltpu.HBM)
    bf16, f32, dma = jnp.bfloat16, jnp.float32, pltpu.SemaphoreType.DMA
    return pl.pallas_call(
        kernel,
        out_shape=jax.ShapeDtypeStruct((ROWS, W), f32),
        in_specs=[hbm] * 6,
        out_specs=pl.BlockSpec(memory_space=pltpu.VMEM),
        scratch_shapes=[
            pltpu.VMEM((W, 2 * W), bf16),
            pltpu.VMEM((2 * W, W), bf16),
            pltpu.VMEM((2, ROOMS, 8, SUB, 128), bf16),
            pltpu.VMEM((NONE + 1, 3, 8, 128), f32),
            pltpu.VMEM((128, 128), f32),
            pltpu.VMEM((PAIRS, 2, ROWS, W), bf16),
            pltpu.VMEM((SPAN * SUB, 128), f32),
            pltpu.VMEM((SPAN * SUB, 128), f32),
            pltpu.VMEM((OUT * SUB, 128), f32),
            pltpu.VMEM((8, ROWS, W), bf16),
            pltpu.VMEM((CHIPS, ROWS, W), bf16),
            pltpu.VMEM((8, 128), jnp.int32),
            pltpu.VMEM((8, 128), f32),
            pltpu.SMEM((8, 128), jnp.int32),
            pltpu.SMEM((8, 128), f32),
            pltpu.SMEM((ROOMS,), jnp.int32),
            pltpu.SMEM((ROOMS,), jnp.int32),
            dma((4,)),
            dma((2,)),
            dma,
            dma,
            dma,
            dma((PAIRS, 2)),
            dma((PAIRS, 2)),
            dma((8,)),
            dma((CHIPS,)),
        ],
        compiler_params=pltpu.CompilerParams(
            collective_id=0, has_side_effects=True, vmem_limit_bytes=67_043_328
        ),
    )(samples, ir, clip_lengths, room_ids, forward_half(W), inverse_table(W))


def solution(mesh):
    in_specs = (P(("tile", "ir"), None), P(None, "ir", None, None), P(), P())
    out_specs = P(("tile", "ir"), None)
    return jax.shard_map(
        on_device, mesh=mesh, in_specs=in_specs, out_specs=out_specs, check_vma=False
    )
```

```python
import jax
import jax.numpy as jnp
import numpy as np
from jax import lax
from jax.experimental import pallas as pl
from jax.experimental.pallas import tpu as pltpu
from jax.sharding import PartitionSpec as P

MESH = pl.DeviceIdType.MESH
W = 1024
ROWS = 8
CHIPS = 8
ROOMS = 16
PARTS = 16
OUT = 64
PAIRS = 5
SPAN = PAIRS * 2 * ROWS
SUB = 2 * W // 128
NONE = ROOMS * PARTS


def forward_part(width):
    length = 2 * width
    sample = np.arange(width // 2)
    bins = np.arange(width)
    phase = sample[:, None] * bins[None, :] % length
    angle = phase * (2.0 * np.pi / length)
    parity = np.where(sample % 2 == 0, 1.0, -1.0)
    sines = np.where(bins[None, :] == 0, parity[:, None], -np.sin(angle))
    table = np.concatenate([np.cos(angle), sines], axis=1)
    return jnp.asarray(table, dtype=jnp.float32).astype(jnp.bfloat16)


def inverse_part(width):
    length = 2 * width
    bins = np.arange(width)
    outputs = width + np.arange(width // 2)
    phase = bins[:, None] * outputs[None, :] % length
    angle = phase * (2.0 * np.pi / length)
    weight = np.where(bins == 0, 1.0, 2.0)[:, None] / length
    parity = np.where(outputs % 2 == 0, 1.0, -1.0)[None, :] / length
    cosines = weight * np.cos(angle)
    sines = np.where(bins[:, None] == 0, parity, -weight * np.sin(angle))
    table = np.concatenate([cosines, sines], axis=0)
    return jnp.asarray(table, dtype=jnp.float32).astype(jnp.bfloat16)


def kernel(
    samples,
    ir,
    lengths,
    rooms,
    forward,
    inverse,
    out,
    fwd_v,
    inv_v,
    ir_v,
    filters,
    unpacked,
    held,
    raw,
    spectra,
    last,
    summed,
    parts_out,
    arrived,
    choice_v,
    first_v,
    choice,
    first,
    lengths_s,
    rooms_s,
    small_sem,
    table_sem,
    ir_send,
    ir_recv,
    ir_own,
    in_send,
    in_recv,
    out_send,
    out_recv,
):
    tile, ir_at = lax.axis_index("tile"), lax.axis_index("ir")
    tiles = lax.axis_size("tile")
    z, c = ir_at // 2, ir_at % 2
    half = z // 4
    other = 2 * z + 1 - c
    far_first = (4, 3, 5, 2, 6, 1, 7, 0)

    get_lengths = pltpu.make_async_copy(lengths, lengths_s, small_sem.at[0])
    get_rooms = pltpu.make_async_copy(rooms, rooms_s, small_sem.at[1])
    get_lengths.start()
    get_rooms.start()

    @pl.when(tile == 0)
    def _():
        held[...] = jnp.zeros(held.shape, held.dtype)

    barrier = pltpu.get_barrier_semaphore()

    def greet(to):
        pl.semaphore_signal(barrier, inc=1, device_id=to, device_id_type=MESH)

    for away in far_first:
        e = (2 * z + away + 9 - 4 * c) % 8
        before = (4 * c + e < z + 1).astype(jnp.int32)
        at = (z + away) % 8
        for k in range(2):
            real = (e < PAIRS) & ((before == 0) | (tile > 0))
            if away == 0:
                real = real & ((before == 1) | (c != k))

            @pl.when(real)
            def _(before=before, at=at, k=k):
                greet(((tile + tiles - before) % tiles, 2 * at + k))

        if away == 0:

            @pl.when(half != c)
            def _(at=at):
                greet((tile, 2 * at + half))

        else:
            greet((tile, 2 * at + half))
    greet((tile, other))

    get_own = pltpu.make_async_copy(ir, ir_v.at[c], ir_own)
    get_own.start()
    get_forward = pltpu.make_async_copy(forward, fwd_v, table_sem.at[0])
    get_forward.start()
    get_inverse = pltpu.make_async_copy(inverse, inv_v, table_sem.at[1])
    get_inverse.start()

    get_lengths.wait()
    get_rooms.wait()
    place = lax.broadcasted_iota(jnp.int32, (8, 128), 0) * 128 + lax.broadcasted_iota(
        jnp.int32, (8, 128), 1
    )
    block = tile * (2 * OUT) + c * OUT + place // PARTS
    delay = z * PARTS + place % PARTS
    row_block = tile * (2 * OUT) + c * OUT - z * PARTS - PARTS + place
    begin = jnp.zeros((8, 128), jnp.int32)
    room = jnp.zeros((8, 128), jnp.int32)
    joined = jnp.ones((8, 128), jnp.float32)
    start = jnp.int32(0)
    for n in range(ROOMS):
        end = start + lengths_s[n]
        member = (block >= start) & (block < end)
        begin = jnp.where(member, start, begin)
        room = jnp.where(member, rooms_s[n], room)
        joined = jnp.where(row_block == start, 0.0, joined)
        start = end
    chosen = jnp.where(block - delay >= begin, room * PARTS + place % PARTS, NONE)
    choice_v[...] = chosen
    first_v[...] = joined
    put_choice = pltpu.make_async_copy(choice_v, choice, small_sem.at[2])
    put_first = pltpu.make_async_copy(first_v, first, small_sem.at[3])
    put_choice.start()
    put_first.start()

    corner = (lax.broadcasted_iota(jnp.int32, (8, 128), 0) == 0) & (
        lax.broadcasted_iota(jnp.int32, (8, 128), 1) == 0
    )
    filters[NONE] = jnp.zeros((3, 8, 128), jnp.float32)

    def unpack(part):
        def step(n, _):
            for p in range(8):
                unpacked[pl.ds(16 * p, 16), :] = ir_v[part, n, p].astype(jnp.float32)
            for p in range(8):
                hre = unpacked[pl.ds(16 * p, 8, stride=2), :]
                him = unpacked[pl.ds(16 * p + 1, 8, stride=2), :]
                at = n * PARTS + part * 8 + p
                filters[at, 0] = hre
                filters[at, 1] = jnp.where(corner, 0.0, him)
                filters[at, 2] = jnp.where(corner, him, hre)
            return 0

        lax.fori_loop(0, ROOMS, step, 0)

    get_own.wait()
    unpack(c)
    last[...] = jnp.zeros(last.shape, jnp.float32)

    own_is_in = ((c == z // 2) & (z < 4)).astype(jnp.int32)
    own_is_out = (half == c).astype(jnp.int32)
    crossing = jnp.minimum(z + 1, PAIRS) + jnp.maximum(z - 3, 0)
    crossing = crossing * (tile == tiles - 1).astype(jnp.int32)
    pl.semaphore_wait(barrier, 2 * PAIRS + CHIPS + 1 - own_is_in - own_is_out - crossing)

    def send_samples(e, d):
        ahead = (4 * d + e < z + 1).astype(jnp.int32)

        @pl.when((ahead == 0) | (tile < tiles - 1))
        def _():
            pltpu.make_async_remote_copy(
                src_ref=samples,
                dst_ref=held.at[e, c],
                send_sem=in_send.at[e, d],
                recv_sem=in_recv.at[e, c],
                device_id=((tile + ahead) % tiles, 2 * ((4 * d + e + 7 - z) % 8) + d),
                device_id_type=MESH,
            ).start()

    for away in far_first:
        place_on_ring = (2 * z + away) % 8
        d, e = place_on_ring // 4, place_on_ring % 4 + 1
        if away == 0:
            itself = own_is_in == 1

            @pl.when(itself)
            def _(e=e):
                pltpu.make_async_copy(samples, held.at[e, c], in_recv.at[e, c]).start()

            @pl.when(jnp.logical_not(itself))
            def _(e=e, d=d):
                send_samples(e, d)

        else:
            send_samples(e, d)

        @pl.when(e == 4)
        def _(d=d):
            send_samples(0, 1 - d)

    send_ir = pltpu.make_async_remote_copy(
        src_ref=ir,
        dst_ref=ir_v.at[c],
        send_sem=ir_send,
        recv_sem=ir_recv,
        device_id=(tile, other),
        device_id_type=MESH,
    )
    send_ir.start()

    put_choice.wait()
    put_first.wait()
    get_forward.wait()
    get_inverse.wait()
    send_ir.wait_recv()
    unpack(1 - c)

    lane = lax.broadcasted_iota(jnp.int32, (8, 128), 1) % 4
    turn_re = jnp.where(lane == 0, 1.0, jnp.where(lane == 2, -1.0, 0.0))
    turn_im = jnp.where(lane == 1, 1.0, jnp.where(lane == 3, -1.0, 0.0))
    sign = 1.0 - 2.0 * (lane % 2).astype(jnp.float32)

    def pair(e, _):
        @pl.when((tile > 0) | (4 * c + e >= z + 1))
        def _():
            for k in range(2):
                pltpu.make_async_copy(samples, held.at[e, k], in_recv.at[e, k]).wait()

        x = held[e].astype(jnp.float32).reshape(16, W)
        x = jnp.concatenate([x[:, : W // 2], x[:, W // 2 :]], axis=0).astype(jnp.bfloat16)
        for n in range(2 * W // 256):
            g = jnp.dot(x, fwd_v[:, 256 * n : 256 * n + 256], preferred_element_type=jnp.float32)
            raw[pl.ds(2 * n, 32, stride=SUB), :] = g[:, :128]
            raw[pl.ds(2 * n + 1, 32, stride=SUB), :] = g[:, 128:]
        before_re, before_im = last[0], last[1]
        for r in range(16):
            first_re, first_im = raw[SUB * r : SUB * r + 8, :], raw[SUB * r + 8 : SUB * r + 16, :]
            at = SUB * (16 + r)
            then_re, then_im = raw[at : at + 8, :], raw[at + 8 : at + 16, :]
            own_re = first_re + (turn_re * then_re + turn_im * then_im)
            own_im = first_im + (turn_re * then_im - turn_im * then_re)
            opens = first[e // 8, 16 * e + r]
            frame_re = opens * before_re + sign * own_re
            frame_im = opens * before_im + sign * own_im
            to = pl.multiple_of(SUB * (16 * e + r), 8)
            spectra[pl.ds(to, 8), :] = frame_re.astype(jnp.bfloat16).astype(jnp.float32)
            spectra[pl.ds(to + 8, 8), :] = frame_im.astype(jnp.bfloat16).astype(jnp.float32)
            before_re, before_im = own_re, own_im
        last[0] = before_re
        last[1] = before_im

        @pl.when(e > 0)
        def _():
            g = e - 1

            def eight(b, _):
                res = [jnp.zeros((8, 128), jnp.float32) for _ in range(8)]
                ims = [jnp.zeros((8, 128), jnp.float32) for _ in range(8)]
                for p in range(PARTS):
                    for t in range(8):
                        at = pl.multiple_of(SUB * (16 * g + 8 * b + t - p + PARTS), 8)
                        are = spectra[pl.ds(at, 8), :]
                        aim = spectra[pl.ds(at + 8, 8), :]
                        h = choice[2 * g + b, 16 * t + p]
                        h0, h1, h2 = filters[h, 0], filters[h, 1], filters[h, 2]
                        res[t] = res[t] + (are * h0 - aim * h1)
                        ims[t] = ims[t] + (are * h1 + aim * h2)
                for t in range(8):
                    to = pl.multiple_of(SUB * (8 * b + t), 8)
                    summed[pl.ds(to, 8), :] = res[t]
                    summed[pl.ds(to + 8, 8), :] = ims[t]
                    summed[pl.ds(16 * SUB + to, 8), :] = turn_re * res[t] - turn_im * ims[t]
                    summed[pl.ds(16 * SUB + to + 8, 8), :] = turn_re * ims[t] + turn_im * res[t]
                return 0

            lax.fori_loop(0, 2, eight, 0)

            y = jnp.concatenate(
                [summed[pl.ds(j, 32, stride=SUB), :].astype(jnp.bfloat16) for j in range(SUB)],
                axis=1,
            )
            for n in range(W // 512):
                v = jnp.dot(
                    y, inv_v[:, 256 * n : 256 * n + 256], preferred_element_type=jnp.float32
                )
                for q in range(4):
                    left = 512 * (q // 2) + 256 * n
                    parts_out[2 * g + q % 2, :, left : left + 256] = v[8 * q : 8 * q + 8].astype(
                        jnp.bfloat16
                    )
            for k in range(2):
                itself = (z == 4 * c + g) & (c == k)

                @pl.when(itself)
                def _(k=k):
                    pltpu.make_async_copy(
                        parts_out.at[2 * g + k], arrived.at[z], out_recv.at[z]
                    ).start()

                @pl.when(jnp.logical_not(itself))
                def _(k=k):
                    pltpu.make_async_remote_copy(
                        src_ref=parts_out.at[2 * g + k],
                        dst_ref=arrived.at[z],
                        send_sem=out_send.at[2 * g + k],
                        recv_sem=out_recv.at[z],
                        device_id=(tile, 2 * (4 * c + g) + k),
                        device_id_type=MESH,
                    ).start()

        return 0

    lax.fori_loop(0, PAIRS, pair, 0)

    send_ir.wait_send()
    for e in range(PAIRS):
        for d in range(2):
            itself = (own_is_in == 1) & (4 * d + e == 2 * z + 1) & (c == d)
            crosses = (4 * d + e < z + 1) & (tile == tiles - 1)

            @pl.when(jnp.logical_not(itself | crosses))
            def _(e=e, d=d):
                pltpu.make_async_copy(samples, held.at[e, 0], in_send.at[e, d]).wait()

    for g in range(4):
        for k in range(2):

            @pl.when(jnp.logical_not((z == 4 * c + g) & (c == k)))
            def _(g=g, k=k):
                pltpu.make_async_copy(
                    parts_out.at[2 * g + k], arrived.at[0], out_send.at[2 * g + k]
                ).wait()

    total = jnp.zeros((ROWS, W), jnp.float32)
    for zs in range(CHIPS):
        pltpu.make_async_copy(parts_out.at[0], arrived.at[zs], out_recv.at[zs]).wait()
        total = total + arrived[zs].astype(jnp.float32)
    out[...] = total


def on_device(samples, ir_spectra, clip_lengths, room_ids):
    rooms, parts = ir_spectra.shape[0], ir_spectra.shape[1]
    ir = ir_spectra.reshape(rooms, parts, 2, W // 128, 128)
    ir = ir.transpose(0, 1, 3, 2, 4).reshape(rooms, parts, SUB, 128)
    hbm = pl.BlockSpec(memory_space=pltpu.HBM)
    bf16, f32, dma = jnp.bfloat16, jnp.float32, pltpu.SemaphoreType.DMA
    return pl.pallas_call(
        kernel,
        out_shape=jax.ShapeDtypeStruct((ROWS, W), f32),
        in_specs=[hbm] * 6,
        out_specs=pl.BlockSpec(memory_space=pltpu.VMEM),
        scratch_shapes=[
            pltpu.VMEM((W // 2, 2 * W), bf16),
            pltpu.VMEM((2 * W, W // 2), bf16),
            pltpu.VMEM((2, ROOMS, 8, SUB, 128), bf16),
            pltpu.VMEM((NONE + 1, 3, 8, 128), f32),
            pltpu.VMEM((128, 128), f32),
            pltpu.VMEM((PAIRS, 2, ROWS, W), bf16),
            pltpu.VMEM((32 * SUB, 128), f32),
            pltpu.VMEM((SPAN * SUB, 128), f32),
            pltpu.VMEM((2, 8, 128), f32),
            pltpu.VMEM((32 * SUB, 128), f32),
            pltpu.VMEM((8, ROWS, W), bf16),
            pltpu.VMEM((CHIPS, ROWS, W), bf16),
            pltpu.VMEM((8, 128), jnp.int32),
            pltpu.VMEM((8, 128), f32),
            pltpu.SMEM((8, 128), jnp.int32),
            pltpu.SMEM((8, 128), f32),
            pltpu.SMEM((ROOMS,), jnp.int32),
            pltpu.SMEM((ROOMS,), jnp.int32),
            dma((4,)),
            dma((2,)),
            dma,
            dma,
            dma,
            dma((PAIRS, 2)),
            dma((PAIRS, 2)),
            dma((8,)),
            dma((CHIPS,)),
        ],
        compiler_params=pltpu.CompilerParams(
            collective_id=0, has_side_effects=True, vmem_limit_bytes=67_043_328
        ),
    )(samples, ir, clip_lengths, room_ids, forward_part(W), inverse_part(W))


def solution(mesh):
    in_specs = (P(("tile", "ir"), None), P(None, "ir", None, None), P(), P())
    out_specs = P(("tile", "ir"), None)
    return jax.shard_map(
        on_device, mesh=mesh, in_specs=in_specs, out_specs=out_specs, check_vma=False
    )
```

```python
import jax
import jax.numpy as jnp
import numpy as np
from jax import lax
from jax.experimental import pallas as pl
from jax.experimental.pallas import tpu as pltpu
from jax.sharding import PartitionSpec as P

MESH = pl.DeviceIdType.MESH
W = 1024
ROWS = 8
CHIPS = 8
ROOMS = 16
PARTS = 16
OUT = 64
PAIRS = 5
SPAN = PAIRS * 2 * ROWS
SUB = 2 * W // 128
NONE = ROOMS * PARTS


def forward_part(width):
    length = 2 * width
    sample = np.arange(width // 2)
    bins = np.arange(width)
    phase = sample[:, None] * bins[None, :] % length
    angle = phase * (2.0 * np.pi / length)
    parity = np.where(sample % 2 == 0, 1.0, -1.0)
    sines = np.where(bins[None, :] == 0, parity[:, None], -np.sin(angle))
    table = np.concatenate([np.cos(angle), sines], axis=1)
    return jnp.asarray(table, dtype=jnp.float32).astype(jnp.bfloat16)


def inverse_part(width):
    length = 2 * width
    bins = np.arange(width)
    outputs = width + np.arange(width // 2)
    phase = bins[:, None] * outputs[None, :] % length
    angle = phase * (2.0 * np.pi / length)
    weight = np.where(bins == 0, 1.0, 2.0)[:, None] / length
    parity = np.where(outputs % 2 == 0, 1.0, -1.0)[None, :] / length
    cosines = weight * np.cos(angle)
    sines = np.where(bins[:, None] == 0, parity, -weight * np.sin(angle))
    table = np.concatenate([cosines, sines], axis=0)
    return jnp.asarray(table, dtype=jnp.float32).astype(jnp.bfloat16)


def kernel(
    samples,
    ir,
    lengths,
    rooms,
    forward,
    inverse,
    out,
    fwd_v,
    inv_v,
    ir_v,
    filters,
    unpacked,
    held,
    raw,
    spectra,
    edges_v,
    summed,
    parts_out,
    arrived,
    out_v,
    choice_v,
    first_v,
    choice,
    first,
    lengths_s,
    rooms_s,
    small_sem,
    table_sem,
    ir_send,
    ir_recv,
    ir_own,
    in_send,
    in_recv,
    out_send,
    out_recv,
):
    tile, ir_at = lax.axis_index("tile"), lax.axis_index("ir")
    tiles = lax.axis_size("tile")
    z, c = ir_at // 2, ir_at % 2
    upper = z // 4
    turn = z - 4 * upper
    other = 2 * z + 1 - c
    far_first = (4, 3, 5, 2, 6, 1, 7, 0)

    get_lengths = pltpu.make_async_copy(lengths, lengths_s, small_sem.at[0])
    get_rooms = pltpu.make_async_copy(rooms, rooms_s, small_sem.at[1])
    get_lengths.start()
    get_rooms.start()

    @pl.when(tile == 0)
    def _():
        held[...] = jnp.zeros(held.shape, held.dtype)
        arrived[...] = jnp.zeros(arrived.shape, arrived.dtype)

    barrier = pltpu.get_barrier_semaphore()

    def flag(x):
        return x.astype(jnp.int32)

    def greet(to):
        pl.semaphore_signal(barrier, inc=1, device_id=to, device_id_type=MESH)

    def sum_source(at):
        from_upper = at // 4
        before = from_upper * (1 - upper)
        core = upper + from_upper * (1 - 2 * upper)
        real = ((before == 0) | (tile > 0)) & ((at != z) | (before == 1) | (core != c))
        return (tile - before, 2 * at + core), real

    for away in far_first:
        at = (z + away) % 8
        e = (z + turn + away + 9 - 4 * c) % 8
        before = flag(4 * c + e < turn + 1)
        for k in range(2):
            real = (e < PAIRS) & ((before == 0) | (tile > 0))
            if away == 0:
                real = real & ((before == 1) | (c != k))

            @pl.when(real)
            def _(before=before, at=at, k=k):
                greet((tile - before, 2 * at + k))

        to, real = sum_source(at)

        @pl.when(real)
        def _(to=to):
            greet(to)

    greet((tile, other))

    get_own = pltpu.make_async_copy(ir, ir_v.at[c], ir_own)
    get_own.start()
    get_forward = pltpu.make_async_copy(forward, fwd_v, table_sem.at[0])
    get_forward.start()
    get_inverse = pltpu.make_async_copy(inverse, inv_v, table_sem.at[1])
    get_inverse.start()

    def sample_target(away, d):
        at = (z + away) % 8
        back = at - 4 * (at // 4)
        e = (z + back + 9 - 4 * d) % 8
        ahead = flag(4 * d + e < back + 1)
        there = (e < PAIRS) & ((ahead == 0) | (tile < tiles - 1))
        itself = (away == 0) & (e < PAIRS) & (ahead == 0) & (d == c)
        return at, e, ahead, there, itself

    def sum_target(g, k):
        ahead = upper * c
        at = 4 * (upper + c - 2 * ahead) + g
        there = (ahead == 0) | (tile < tiles - 1)
        itself = (ahead == 0) & (at == z) & (k == c)
        return (tile + ahead, 2 * at + k), there, itself

    awaited = jnp.int32(1)
    for away in range(CHIPS):
        for d in range(2):
            _, _, _, there, itself = sample_target(away, d)
            awaited = awaited + flag(there & jnp.logical_not(itself))
    for g in range(4):
        for k in range(2):
            _, there, itself = sum_target(g, k)
            awaited = awaited + flag(there & jnp.logical_not(itself))
    pl.semaphore_wait(barrier, awaited)

    for away in far_first[::-1]:
        for d in range(2):
            at, e, ahead, there, itself = sample_target(away, d)
            if away == 0:

                @pl.when(itself)
                def _(e=e):
                    pltpu.make_async_copy(samples, held.at[e, c], in_recv.at[e, c]).start()

            @pl.when(there & jnp.logical_not(itself))
            def _(at=at, e=e, ahead=ahead, away=away, d=d):
                pltpu.make_async_remote_copy(
                    src_ref=samples,
                    dst_ref=held.at[e, c],
                    send_sem=in_send.at[away, d],
                    recv_sem=in_recv.at[e, c],
                    device_id=(tile + ahead, 2 * at + d),
                    device_id_type=MESH,
                ).start()

    send_ir = pltpu.make_async_remote_copy(
        src_ref=ir,
        dst_ref=ir_v.at[c],
        send_sem=ir_send,
        recv_sem=ir_recv,
        device_id=(tile, other),
        device_id_type=MESH,
    )
    send_ir.start()

    get_lengths.wait()
    get_rooms.wait()
    place = lax.broadcasted_iota(jnp.int32, (8, 128), 0) * 128 + lax.broadcasted_iota(
        jnp.int32, (8, 128), 1
    )
    base = tile * (2 * OUT) + (upper + c) * OUT
    block = base + place // PARTS
    delay = z * PARTS + place % PARTS
    row_block = base - z * PARTS - PARTS + place
    begin = jnp.zeros((8, 128), jnp.int32)
    room = jnp.zeros((8, 128), jnp.int32)
    joined = jnp.ones((8, 128), jnp.float32)
    start = jnp.int32(0)
    for n in range(ROOMS):
        end = start + lengths_s[n]
        member = (block >= start) & (block < end)
        begin = jnp.where(member, start, begin)
        room = jnp.where(member, rooms_s[n], room)
        joined = jnp.where(row_block == start, 0.0, joined)
        start = end
    chosen = jnp.where(block - delay >= begin, room * PARTS + place % PARTS, NONE)
    choice_v[...] = chosen
    first_v[...] = joined
    put_choice = pltpu.make_async_copy(choice_v, choice, small_sem.at[2])
    put_first = pltpu.make_async_copy(first_v, first, small_sem.at[3])
    put_choice.start()
    put_first.start()

    corner = (lax.broadcasted_iota(jnp.int32, (8, 128), 0) == 0) & (
        lax.broadcasted_iota(jnp.int32, (8, 128), 1) == 0
    )
    filters[NONE] = jnp.zeros((3, 8, 128), jnp.float32)

    def unpack(part):
        def step(n, _):
            for p in range(8):
                unpacked[pl.ds(16 * p, 16), :] = ir_v[part, n, p].astype(jnp.float32)
            for p in range(8):
                hre = unpacked[pl.ds(16 * p, 8, stride=2), :]
                him = unpacked[pl.ds(16 * p + 1, 8, stride=2), :]
                at = n * PARTS + part * 8 + p
                filters[at, 0] = hre
                filters[at, 1] = jnp.where(corner, 0.0, him)
                filters[at, 2] = jnp.where(corner, him, hre)
            return 0

        lax.fori_loop(0, ROOMS, step, 0)

    get_own.wait()
    unpack(c)

    put_choice.wait()
    put_first.wait()
    get_forward.wait()
    get_inverse.wait()
    send_ir.wait_recv()
    unpack(1 - c)

    lane = lax.broadcasted_iota(jnp.int32, (8, 128), 1) % 4
    turn_re = jnp.where(lane == 0, 1.0, jnp.where(lane == 2, -1.0, 0.0))
    turn_im = jnp.where(lane == 1, 1.0, jnp.where(lane == 3, -1.0, 0.0))
    sign = 1.0 - 2.0 * (lane % 2).astype(jnp.float32)

    down = ((z + 4 - 2 * (upper + c)) % 4 + 1) // 2 % 2

    def frame(row, opens, before_re, before_im, own_re, own_im):
        frame_re = opens * before_re + sign * own_re
        frame_im = opens * before_im + sign * own_im
        to = pl.multiple_of(SUB * row, 8)
        spectra[pl.ds(to, 8), :] = frame_re.astype(jnp.bfloat16).astype(jnp.float32)
        spectra[pl.ds(to + 8, 8), :] = frame_im.astype(jnp.bfloat16).astype(jnp.float32)

    def pair(step, _):
        e = step + down * (PAIRS - 1 - 2 * step)

        @pl.when((tile > 0) | (4 * c + e >= turn + 1))
        def _():
            for k in range(2):
                pltpu.make_async_copy(samples, held.at[e, k], in_recv.at[e, k]).wait()

        x = held[e].astype(jnp.float32).reshape(16, W)
        x = jnp.concatenate([x[:, : W // 2], x[:, W // 2 :]], axis=0).astype(jnp.bfloat16)
        for n in range(2 * W // 256):
            g = jnp.dot(x, fwd_v[:, 256 * n : 256 * n + 256], preferred_element_type=jnp.float32)
            raw[pl.ds(2 * n, 32, stride=SUB), :] = g[:, :128]
            raw[pl.ds(2 * n + 1, 32, stride=SUB), :] = g[:, 128:]
        before_re, before_im = None, None
        for r in range(16):
            first_re, first_im = raw[SUB * r : SUB * r + 8, :], raw[SUB * r + 8 : SUB * r + 16, :]
            at = SUB * (16 + r)
            then_re, then_im = raw[at : at + 8, :], raw[at + 8 : at + 16, :]
            own_re = first_re + (turn_re * then_re + turn_im * then_im)
            own_im = first_im + (turn_re * then_im - turn_im * then_re)
            if r == 0:
                edges_v[e, 0, 0] = own_re
                edges_v[e, 0, 1] = own_im
            else:
                frame(16 * e + r, first[0, 16 * e + r], before_re, before_im, own_re, own_im)
            before_re, before_im = own_re, own_im
        edges_v[e, 1, 0] = before_re
        edges_v[e, 1, 1] = before_im

        @pl.when((step == 2) | (step == 4))
        def _():
            h32 = flag(step == 2 + 2 * (1 - down))
            for n in range(2):
                b = 2 * h32 + n
                row = 16 * b + 16
                tail_re, tail_im = edges_v[b, 1, 0], edges_v[b, 1, 1]
                head_re, head_im = edges_v[b + 1, 0, 0], edges_v[b + 1, 0, 1]
                frame(row, first[0, row], tail_re, tail_im, head_re, head_im)

            def eight(b, _):
                res = [jnp.zeros((8, 128), jnp.float32) for _ in range(8)]
                ims = [jnp.zeros((8, 128), jnp.float32) for _ in range(8)]
                for p in range(PARTS):
                    for t in range(8):
                        at = pl.multiple_of(SUB * (32 * h32 + 8 * b + t - p + PARTS), 8)
                        are = spectra[pl.ds(at, 8), :]
                        aim = spectra[pl.ds(at + 8, 8), :]
                        h = choice[4 * h32 + b, 16 * t + p]
                        h0, h1, h2 = filters[h, 0], filters[h, 1], filters[h, 2]
                        res[t] = res[t] + (are * h0 - aim * h1)
                        ims[t] = ims[t] + (are * h1 + aim * h2)
                for t in range(8):
                    to = pl.multiple_of(SUB * (8 * b + t), 8)
                    summed[pl.ds(to, 8), :] = res[t]
                    summed[pl.ds(to + 8, 8), :] = ims[t]
                    summed[pl.ds(32 * SUB + to, 8), :] = turn_re * res[t] - turn_im * ims[t]
                    summed[pl.ds(32 * SUB + to + 8, 8), :] = turn_re * ims[t] + turn_im * res[t]
                return 0

            lax.fori_loop(0, 4, eight, 0)

            y = jnp.concatenate(
                [summed[pl.ds(j, 64, stride=SUB), :].astype(jnp.bfloat16) for j in range(SUB)],
                axis=1,
            )
            for n in range(W // 512):
                v = jnp.dot(
                    y, inv_v[:, 256 * n : 256 * n + 256], preferred_element_type=jnp.float32
                )
                for q in range(8):
                    left = 512 * (q // 4) + 256 * n
                    parts_out[4 * h32 + q % 4, :, left : left + 256] = v[8 * q : 8 * q + 8].astype(
                        jnp.bfloat16
                    )
            for in_half in range(2):
                g = 2 * h32 + in_half
                for k in range(2):
                    to, there, itself = sum_target(g, k)

                    @pl.when(itself)
                    def _(k=k, g=g):
                        pltpu.make_async_copy(
                            parts_out.at[2 * g + k], arrived.at[z], out_recv.at[z]
                        ).start()

                    @pl.when(there & jnp.logical_not(itself))
                    def _(k=k, g=g, to=to):
                        pltpu.make_async_remote_copy(
                            src_ref=parts_out.at[2 * g + k],
                            dst_ref=arrived.at[z],
                            send_sem=out_send.at[2 * g + k],
                            recv_sem=out_recv.at[z],
                            device_id=to,
                            device_id_type=MESH,
                        ).start()

        return 0

    lax.fori_loop(0, PAIRS, pair, 0)

    total = jnp.zeros((ROWS, W), jnp.float32)
    for zs in range(CHIPS):

        @pl.when((tile > 0) | (upper == 1) | (zs < 4))
        def _(zs=zs):
            pltpu.make_async_copy(parts_out.at[0], arrived.at[zs], out_recv.at[zs]).wait()

        total = total + arrived[zs].astype(jnp.float32)
    out_v[...] = total
    put_out = pltpu.make_async_copy(out_v, out, small_sem.at[2])
    put_out.start()

    send_ir.wait_send()
    for away in range(CHIPS):
        for d in range(2):
            _, _, _, there, itself = sample_target(away, d)

            @pl.when(there & jnp.logical_not(itself))
            def _(away=away, d=d):
                pltpu.make_async_copy(samples, held.at[0, 0], in_send.at[away, d]).wait()

    for g in range(4):
        for k in range(2):
            _, there, itself = sum_target(g, k)

            @pl.when(there & jnp.logical_not(itself))
            def _(g=g, k=k):
                pltpu.make_async_copy(
                    parts_out.at[2 * g + k], arrived.at[0], out_send.at[2 * g + k]
                ).wait()

    put_out.wait()


def on_device(samples, ir_spectra, clip_lengths, room_ids):
    rooms, parts = ir_spectra.shape[0], ir_spectra.shape[1]
    ir = ir_spectra.reshape(rooms, parts, 2, W // 128, 128)
    ir = ir.transpose(0, 1, 3, 2, 4).reshape(rooms, parts, SUB, 128)
    hbm = pl.BlockSpec(memory_space=pltpu.HBM)
    bf16, f32, dma = jnp.bfloat16, jnp.float32, pltpu.SemaphoreType.DMA
    return pl.pallas_call(
        kernel,
        out_shape=jax.ShapeDtypeStruct((ROWS, W), f32),
        in_specs=[hbm] * 6,
        out_specs=pl.BlockSpec(memory_space=pltpu.HBM),
        scratch_shapes=[
            pltpu.VMEM((W // 2, 2 * W), bf16),
            pltpu.VMEM((2 * W, W // 2), bf16),
            pltpu.VMEM((2, ROOMS, 8, SUB, 128), bf16),
            pltpu.VMEM((NONE + 1, 3, 8, 128), f32),
            pltpu.VMEM((128, 128), f32),
            pltpu.VMEM((PAIRS, 2, ROWS, W), bf16),
            pltpu.VMEM((32 * SUB, 128), f32),
            pltpu.VMEM((SPAN * SUB, 128), f32),
            pltpu.VMEM((PAIRS, 2, 2, 8, 128), f32),
            pltpu.VMEM((64 * SUB, 128), f32),
            pltpu.VMEM((8, ROWS, W), bf16),
            pltpu.VMEM((CHIPS, ROWS, W), bf16),
            pltpu.VMEM((ROWS, W), f32),
            pltpu.VMEM((8, 128), jnp.int32),
            pltpu.VMEM((8, 128), f32),
            pltpu.SMEM((8, 128), jnp.int32),
            pltpu.SMEM((8, 128), f32),
            pltpu.SMEM((ROOMS,), jnp.int32),
            pltpu.SMEM((ROOMS,), jnp.int32),
            dma((4,)),
            dma((2,)),
            dma,
            dma,
            dma,
            dma((CHIPS, 2)),
            dma((PAIRS, 2)),
            dma((8,)),
            dma((CHIPS,)),
        ],
        compiler_params=pltpu.CompilerParams(
            collective_id=0, has_side_effects=True, vmem_limit_bytes=67_043_328
        ),
    )(samples, ir, clip_lengths, room_ids, forward_part(W), inverse_part(W))


def solution(mesh):
    in_specs = (P(("tile", "ir"), None), P(None, "ir", None, None), P(), P())
    out_specs = P(("tile", "ir"), None)
    return jax.shard_map(
        on_device, mesh=mesh, in_specs=in_specs, out_specs=out_specs, check_vma=False
    )
```

```python
import jax
import jax.numpy as jnp
import numpy as np
from jax import lax
from jax.experimental import pallas as pl
from jax.experimental.pallas import tpu as pltpu
from jax.sharding import PartitionSpec as P

MESH = pl.DeviceIdType.MESH
W = 1024
ROWS = 8
CHIPS = 8
ROOMS = 16
PARTS = 16
OUT = 64
PAIRS = 5
SPAN = PAIRS * 2 * ROWS
SUB = 2 * W // 128
NONE = ROOMS * PARTS


def forward_part(width):
    length = 2 * width
    sample = np.arange(width // 2)
    bins = np.arange(width)
    phase = sample[:, None] * bins[None, :] % length
    angle = phase * (2.0 * np.pi / length)
    parity = np.where(sample % 2 == 0, 1.0, -1.0)
    sines = np.where(bins[None, :] == 0, parity[:, None], -np.sin(angle))
    table = np.concatenate([np.cos(angle), sines], axis=1)
    return jnp.asarray(table, dtype=jnp.float32).astype(jnp.bfloat16)


def inverse_part(width):
    length = 2 * width
    bins = np.arange(width)
    outputs = width + np.arange(width // 2)
    phase = bins[:, None] * outputs[None, :] % length
    angle = phase * (2.0 * np.pi / length)
    weight = np.where(bins == 0, 1.0, 2.0)[:, None] / length
    parity = np.where(outputs % 2 == 0, 1.0, -1.0)[None, :] / length
    cosines = weight * np.cos(angle)
    sines = np.where(bins[:, None] == 0, parity, -weight * np.sin(angle))
    table = np.concatenate([cosines, sines], axis=0)
    return jnp.asarray(table, dtype=jnp.float32).astype(jnp.bfloat16)


def kernel(
    samples,
    ir,
    lengths,
    rooms,
    forward,
    inverse,
    arrived,
    fwd_v,
    inv_v,
    ir_v,
    filters,
    unpacked,
    mine,
    held,
    raw,
    spectra,
    edges_v,
    summed,
    parts_out,
    choice_v,
    first_v,
    choice,
    first,
    lengths_s,
    rooms_s,
    small_sem,
    table_sem,
    ir_send,
    ir_recv,
    ir_own,
    in_send,
    in_recv,
    out_send,
    out_recv,
):
    tile, ir_at = lax.axis_index("tile"), lax.axis_index("ir")
    tiles = lax.axis_size("tile")
    z, c = ir_at // 2, ir_at % 2
    upper = z // 4
    turn = z - 4 * upper
    other = 2 * z + 1 - c
    far_first = (4, 3, 5, 2, 6, 1, 7, 0)

    get_lengths = pltpu.make_async_copy(lengths, lengths_s, small_sem.at[0])
    get_rooms = pltpu.make_async_copy(rooms, rooms_s, small_sem.at[1])
    get_samples = pltpu.make_async_copy(samples, mine, small_sem.at[3])
    get_samples.start()
    get_lengths.start()
    get_rooms.start()

    @pl.when(tile == 0)
    def _():
        held[...] = jnp.zeros(held.shape, held.dtype)
        parts_out[...] = jnp.zeros(parts_out.shape, parts_out.dtype)
        clear = pltpu.make_async_copy(parts_out, arrived, small_sem.at[2])
        clear.start()
        clear.wait()

    barrier = pltpu.get_barrier_semaphore()

    def flag(x):
        return x.astype(jnp.int32)

    def greet(to):
        pl.semaphore_signal(barrier, inc=1, device_id=to, device_id_type=MESH)

    def sum_source(at):
        from_upper = at // 4
        before = from_upper * (1 - upper)
        core = upper + from_upper * (1 - 2 * upper)
        real = ((before == 0) | (tile > 0)) & ((at != z) | (before == 1) | (core != c))
        return (tile - before, 2 * at + core), real

    for away in far_first:
        at = (z + away) % 8
        e = (z + turn + away + 9 - 4 * c) % 8
        before = flag(4 * c + e < turn + 1)
        for k in range(2):
            real = (e < PAIRS) & ((before == 0) | (tile > 0))
            if away == 0:
                real = real & ((before == 1) | (c != k))

            @pl.when(real)
            def _(before=before, at=at, k=k):
                greet((tile - before, 2 * at + k))

        to, real = sum_source(at)

        @pl.when(real)
        def _(to=to):
            greet(to)

    greet((tile, other))

    get_own = pltpu.make_async_copy(ir, ir_v.at[c], ir_own)
    get_own.start()
    get_forward = pltpu.make_async_copy(forward, fwd_v, table_sem.at[0])
    get_forward.start()
    get_inverse = pltpu.make_async_copy(inverse, inv_v, table_sem.at[1])
    get_inverse.start()

    def sample_target(away, d):
        at = (z + away) % 8
        back = at - 4 * (at // 4)
        e = (z + back + 9 - 4 * d) % 8
        ahead = flag(4 * d + e < back + 1)
        there = (e < PAIRS) & ((ahead == 0) | (tile < tiles - 1))
        itself = (away == 0) & (e < PAIRS) & (ahead == 0) & (d == c)
        return at, e, ahead, there, itself

    def sum_target(g, k):
        ahead = upper * c
        at = 4 * (upper + c - 2 * ahead) + g
        there = (ahead == 0) | (tile < tiles - 1)
        itself = (ahead == 0) & (at == z) & (k == c)
        return (tile + ahead, 2 * at + k), there, itself

    _, _, _, _, own_is_in = sample_target(0, c)
    _, _, own_is_out = sum_target(z % 4, c)
    last = flag(tile == tiles - 1)
    awaited = 1 + 2 * PAIRS + CHIPS - flag(own_is_in) - flag(own_is_out)
    awaited = awaited - last * (2 * jnp.maximum(z - 3, 0) + 8 * upper * c)
    get_samples.wait()
    pl.semaphore_wait(barrier, awaited)

    for window in range(2):
        for away in far_first[::-1]:
            d = ((z + away) % 8 // 4 + window) % 2
            at, e, ahead, there, itself = sample_target(away, d)
            if away == 0:

                @pl.when(itself)
                def _(e=e):
                    pltpu.make_async_copy(mine, held.at[e, c], in_recv.at[e, c]).start()

            @pl.when(there & jnp.logical_not(itself))
            def _(at=at, e=e, ahead=ahead, away=away, d=d):
                pltpu.make_async_remote_copy(
                    src_ref=mine,
                    dst_ref=held.at[e, c],
                    send_sem=in_send.at[away, d],
                    recv_sem=in_recv.at[e, c],
                    device_id=(tile + ahead, 2 * at + d),
                    device_id_type=MESH,
                ).start()

    send_ir = pltpu.make_async_remote_copy(
        src_ref=ir,
        dst_ref=ir_v.at[c],
        send_sem=ir_send,
        recv_sem=ir_recv,
        device_id=(tile, other),
        device_id_type=MESH,
    )
    send_ir.start()

    get_lengths.wait()
    get_rooms.wait()
    place = lax.broadcasted_iota(jnp.int32, (8, 128), 0) * 128 + lax.broadcasted_iota(
        jnp.int32, (8, 128), 1
    )
    base = tile * (2 * OUT) + (upper + c) * OUT
    block = base + place // PARTS
    delay = z * PARTS + place % PARTS
    row_block = base - z * PARTS - PARTS + place
    begin = jnp.zeros((8, 128), jnp.int32)
    room = jnp.zeros((8, 128), jnp.int32)
    joined = jnp.ones((8, 128), jnp.float32)
    start = jnp.int32(0)
    for n in range(ROOMS):
        end = start + lengths_s[n]
        member = (block >= start) & (block < end)
        begin = jnp.where(member, start, begin)
        room = jnp.where(member, rooms_s[n], room)
        joined = jnp.where(row_block == start, 0.0, joined)
        start = end
    chosen = jnp.where(block - delay >= begin, room * PARTS + place % PARTS, NONE)
    choice_v[...] = chosen
    first_v[...] = joined
    put_choice = pltpu.make_async_copy(choice_v, choice, small_sem.at[2])
    put_first = pltpu.make_async_copy(first_v, first, small_sem.at[3])
    put_choice.start()
    put_first.start()

    corner = (lax.broadcasted_iota(jnp.int32, (8, 128), 0) == 0) & (
        lax.broadcasted_iota(jnp.int32, (8, 128), 1) == 0
    )
    filters[NONE] = jnp.zeros((3, 8, 128), jnp.float32)

    def unpack(part):
        def step(n, _):
            for p in range(8):
                unpacked[pl.ds(16 * p, 16), :] = ir_v[part, n, p].astype(jnp.float32)
            for p in range(8):
                hre = unpacked[pl.ds(16 * p, 8, stride=2), :]
                him = unpacked[pl.ds(16 * p + 1, 8, stride=2), :]
                at = n * PARTS + part * 8 + p
                filters[at, 0] = hre
                filters[at, 1] = jnp.where(corner, 0.0, him)
                filters[at, 2] = jnp.where(corner, him, hre)
            return 0

        lax.fori_loop(0, ROOMS, step, 0)

    get_own.wait()
    unpack(c)

    put_choice.wait()
    put_first.wait()
    get_forward.wait()
    get_inverse.wait()
    send_ir.wait_recv()
    unpack(1 - c)

    lane = lax.broadcasted_iota(jnp.int32, (8, 128), 1) % 4
    turn_re = jnp.where(lane == 0, 1.0, jnp.where(lane == 2, -1.0, 0.0))
    turn_im = jnp.where(lane == 1, 1.0, jnp.where(lane == 3, -1.0, 0.0))
    sign = 1.0 - 2.0 * (lane % 2).astype(jnp.float32)

    down = ((z + 4 - 2 * (upper + c)) % 4 + 1) // 2 % 2
    late = down * ((upper + c + 1) % 2)
    swap = down - late

    def frame(row, opens, before_re, before_im, own_re, own_im):
        frame_re = opens * before_re + sign * own_re
        frame_im = opens * before_im + sign * own_im
        to = pl.multiple_of(SUB * row, 8)
        spectra[pl.ds(to, 8), :] = frame_re.astype(jnp.bfloat16).astype(jnp.float32)
        spectra[pl.ds(to + 8, 8), :] = frame_im.astype(jnp.bfloat16).astype(jnp.float32)

    def pair(step, _):
        e = step + down * (PAIRS - 1 - 2 * step)

        @pl.when((tile > 0) | (4 * c + e >= turn + 1))
        def _():
            for k in range(2):
                pltpu.make_async_copy(samples, held.at[e, k], in_recv.at[e, k]).wait()

        x = held[e].astype(jnp.float32).reshape(16, W)
        x = jnp.concatenate([x[:, : W // 2], x[:, W // 2 :]], axis=0).astype(jnp.bfloat16)
        for n in range(2 * W // 256):
            g = jnp.dot(x, fwd_v[:, 256 * n : 256 * n + 256], preferred_element_type=jnp.float32)
            raw[pl.ds(2 * n, 32, stride=SUB), :] = g[:, :128]
            raw[pl.ds(2 * n + 1, 32, stride=SUB), :] = g[:, 128:]
        before_re, before_im = None, None
        for r in range(16):
            first_re, first_im = raw[SUB * r : SUB * r + 8, :], raw[SUB * r + 8 : SUB * r + 16, :]
            at = SUB * (16 + r)
            then_re, then_im = raw[at : at + 8, :], raw[at + 8 : at + 16, :]
            own_re = first_re + (turn_re * then_re + turn_im * then_im)
            own_im = first_im + (turn_re * then_im - turn_im * then_re)
            if r == 0:
                edges_v[e, 0, 0] = own_re
                edges_v[e, 0, 1] = own_im
            else:
                frame(16 * e + r, first[0, 16 * e + r], before_re, before_im, own_re, own_im)
            before_re, before_im = own_re, own_im
        edges_v[e, 1, 0] = before_re
        edges_v[e, 1, 1] = before_im

        def half_sums(m, _):
            h32 = m + swap * (1 - 2 * m)
            for n in range(2):
                b = 2 * h32 + n
                row = 16 * b + 16
                tail_re, tail_im = edges_v[b, 1, 0], edges_v[b, 1, 1]
                head_re, head_im = edges_v[b + 1, 0, 0], edges_v[b + 1, 0, 1]
                frame(row, first[0, row], tail_re, tail_im, head_re, head_im)

            def eight(b, _):
                res = [jnp.zeros((8, 128), jnp.float32) for _ in range(8)]
                ims = [jnp.zeros((8, 128), jnp.float32) for _ in range(8)]
                for p in range(PARTS):
                    for t in range(8):
                        at = pl.multiple_of(SUB * (32 * h32 + 8 * b + t - p + PARTS), 8)
                        are = spectra[pl.ds(at, 8), :]
                        aim = spectra[pl.ds(at + 8, 8), :]
                        h = choice[4 * h32 + b, 16 * t + p]
                        h0, h1, h2 = filters[h, 0], filters[h, 1], filters[h, 2]
                        res[t] = res[t] + (are * h0 - aim * h1)
                        ims[t] = ims[t] + (are * h1 + aim * h2)
                for t in range(8):
                    to = pl.multiple_of(SUB * (8 * b + t), 8)
                    summed[pl.ds(to, 8), :] = res[t]
                    summed[pl.ds(to + 8, 8), :] = ims[t]
                    summed[pl.ds(32 * SUB + to, 8), :] = turn_re * res[t] - turn_im * ims[t]
                    summed[pl.ds(32 * SUB + to + 8, 8), :] = turn_re * ims[t] + turn_im * res[t]
                return 0

            lax.fori_loop(0, 4, eight, 0)

            y = jnp.concatenate(
                [summed[pl.ds(j, 64, stride=SUB), :].astype(jnp.bfloat16) for j in range(SUB)],
                axis=1,
            )
            for n in range(W // 512):
                v = jnp.dot(
                    y, inv_v[:, 256 * n : 256 * n + 256], preferred_element_type=jnp.float32
                )
                for q in range(8):
                    left = 512 * (q // 4) + 256 * n
                    parts_out[4 * h32 + q % 4, :, left : left + 256] = v[8 * q : 8 * q + 8].astype(
                        jnp.bfloat16
                    )
            for in_half in range(2):
                g = 2 * h32 + in_half
                for k in range(2):
                    to, there, itself = sum_target(g, k)

                    @pl.when(itself)
                    def _(k=k, g=g):
                        pltpu.make_async_copy(
                            parts_out.at[2 * g + k], arrived.at[z], out_recv.at[z]
                        ).start()

                    @pl.when(there & jnp.logical_not(itself))
                    def _(k=k, g=g, to=to):
                        pltpu.make_async_remote_copy(
                            src_ref=parts_out.at[2 * g + k],
                            dst_ref=arrived.at[z],
                            send_sem=out_send.at[2 * g + k],
                            recv_sem=out_recv.at[z],
                            device_id=to,
                            device_id_type=MESH,
                        ).start()

            return 0

        at_third, at_last = flag(step == 2), flag(step == 4)
        begun = at_last * (1 - late)
        lax.fori_loop(begun, at_third * (1 - late) + 2 * at_last, half_sums, 0)
        return 0

    lax.fori_loop(0, PAIRS, pair, 0)

    send_ir.wait_send()
    for away in range(CHIPS):
        for d in range(2):
            _, _, _, there, itself = sample_target(away, d)

            @pl.when(there & jnp.logical_not(itself))
            def _(away=away, d=d):
                pltpu.make_async_copy(samples, held.at[0, 0], in_send.at[away, d]).wait()

    for g in range(4):
        for k in range(2):
            _, there, itself = sum_target(g, k)

            @pl.when(there & jnp.logical_not(itself))
            def _(g=g, k=k):
                pltpu.make_async_copy(
                    parts_out.at[2 * g + k], arrived.at[0], out_send.at[2 * g + k]
                ).wait()

    for zs in range(CHIPS):

        @pl.when((tile > 0) | (upper == 1) | (zs < 4))
        def _(zs=zs):
            pltpu.make_async_copy(parts_out.at[0], arrived.at[zs], out_recv.at[zs]).wait()


def on_device(samples, ir_spectra, clip_lengths, room_ids):
    rooms, parts = ir_spectra.shape[0], ir_spectra.shape[1]
    ir = ir_spectra.reshape(rooms, parts, 2, W // 128, 128)
    ir = ir.transpose(0, 1, 3, 2, 4).reshape(rooms, parts, SUB, 128)
    hbm = pl.BlockSpec(memory_space=pltpu.HBM)
    bf16, f32, dma = jnp.bfloat16, jnp.float32, pltpu.SemaphoreType.DMA
    arrived = pl.pallas_call(
        kernel,
        out_shape=jax.ShapeDtypeStruct((CHIPS, ROWS, W), bf16),
        in_specs=[hbm] * 6,
        out_specs=pl.BlockSpec(memory_space=pltpu.HBM),
        scratch_shapes=[
            pltpu.VMEM((W // 2, 2 * W), bf16),
            pltpu.VMEM((2 * W, W // 2), bf16),
            pltpu.VMEM((2, ROOMS, 8, SUB, 128), bf16),
            pltpu.VMEM((NONE + 1, 3, 8, 128), f32),
            pltpu.VMEM((128, 128), f32),
            pltpu.VMEM((ROWS, W), bf16),
            pltpu.VMEM((PAIRS, 2, ROWS, W), bf16),
            pltpu.VMEM((32 * SUB, 128), f32),
            pltpu.VMEM((SPAN * SUB, 128), f32),
            pltpu.VMEM((PAIRS, 2, 2, 8, 128), f32),
            pltpu.VMEM((64 * SUB, 128), f32),
            pltpu.VMEM((8, ROWS, W), bf16),
            pltpu.VMEM((8, 128), jnp.int32),
            pltpu.VMEM((8, 128), f32),
            pltpu.SMEM((8, 128), jnp.int32),
            pltpu.SMEM((8, 128), f32),
            pltpu.SMEM((ROOMS,), jnp.int32),
            pltpu.SMEM((ROOMS,), jnp.int32),
            dma((4,)),
            dma((2,)),
            dma,
            dma,
            dma,
            dma((CHIPS, 2)),
            dma((PAIRS, 2)),
            dma((8,)),
            dma((CHIPS,)),
        ],
        compiler_params=pltpu.CompilerParams(
            collective_id=0, has_side_effects=True, vmem_limit_bytes=67_043_328
        ),
    )(samples, ir, clip_lengths, room_ids, forward_part(W), inverse_part(W))
    return jnp.sum(arrived.astype(f32), axis=0)


def solution(mesh):
    in_specs = (P(("tile", "ir"), None), P(None, "ir", None, None), P(), P())
    out_specs = P(("tile", "ir"), None)
    return jax.shard_map(
        on_device, mesh=mesh, in_specs=in_specs, out_specs=out_specs, check_vma=False
    )
```

```python
import jax
import jax.numpy as jnp
import numpy as np
from jax import lax
from jax.experimental import pallas as pl
from jax.experimental.pallas import tpu as pltpu
from jax.sharding import PartitionSpec as P

MESH = pl.DeviceIdType.MESH
W = 1024
ROWS = 8
CHIPS = 8
ROOMS = 16
PARTS = 16
OUT = 64
PAIRS = 5
SPAN = PAIRS * 2 * ROWS
SUB = 2 * W // 128
NONE = ROOMS * PARTS


def forward_part(width):
    length = 2 * width
    sample = np.arange(width // 2)
    bins = np.arange(width)
    phase = sample[:, None] * bins[None, :] % length
    angle = phase * (2.0 * np.pi / length)
    parity = np.where(sample % 2 == 0, 1.0, -1.0)
    sines = np.where(bins[None, :] == 0, parity[:, None], -np.sin(angle))
    table = np.concatenate([np.cos(angle), sines], axis=1)
    return jnp.asarray(table, dtype=jnp.float32).astype(jnp.bfloat16)


def inverse_part(width):
    length = 2 * width
    bins = np.arange(width)
    outputs = width + np.arange(width // 2)
    phase = bins[:, None] * outputs[None, :] % length
    angle = phase * (2.0 * np.pi / length)
    weight = np.where(bins == 0, 1.0, 2.0)[:, None] / length
    parity = np.where(outputs % 2 == 0, 1.0, -1.0)[None, :] / length
    cosines = weight * np.cos(angle)
    sines = np.where(bins[:, None] == 0, parity, -weight * np.sin(angle))
    table = np.concatenate([cosines, sines], axis=0)
    return jnp.asarray(table, dtype=jnp.float32).astype(jnp.bfloat16)


def kernel(
    samples,
    ir,
    lengths,
    rooms,
    forward,
    inverse,
    out,
    fwd_v,
    inv_v,
    ir_v,
    filters,
    unpacked,
    mine,
    held,
    raw,
    spectra,
    edges_v,
    summed,
    parts_out,
    arrived,
    choice_v,
    first_v,
    choice,
    first,
    lengths_s,
    rooms_s,
    small_sem,
    table_sem,
    ir_send,
    ir_recv,
    ir_own,
    in_send,
    in_recv,
    out_send,
    out_recv,
):
    tile, ir_at = lax.axis_index("tile"), lax.axis_index("ir")
    tiles = lax.axis_size("tile")
    z, c = ir_at // 2, ir_at % 2
    upper = z // 4
    turn = z - 4 * upper
    other = 2 * z + 1 - c
    far_first = (4, 3, 5, 2, 6, 1, 7, 0)

    get_lengths = pltpu.make_async_copy(lengths, lengths_s, small_sem.at[0])
    get_rooms = pltpu.make_async_copy(rooms, rooms_s, small_sem.at[1])
    get_samples = pltpu.make_async_copy(samples, mine, small_sem.at[3])
    get_samples.start()
    get_lengths.start()
    get_rooms.start()

    @pl.when(tile == 0)
    def _():
        held[...] = jnp.zeros(held.shape, held.dtype)
        arrived[...] = jnp.zeros(arrived.shape, arrived.dtype)

    barrier = pltpu.get_barrier_semaphore()

    def flag(x):
        return x.astype(jnp.int32)

    def greet(to):
        pl.semaphore_signal(barrier, inc=1, device_id=to, device_id_type=MESH)

    def sum_source(at):
        from_upper = at // 4
        before = from_upper * (1 - upper)
        core = upper + from_upper * (1 - 2 * upper)
        real = ((before == 0) | (tile > 0)) & ((at != z) | (before == 1) | (core != c))
        return (tile - before, 2 * at + core), real

    for away in far_first:
        at = (z + away) % 8
        e = (z + turn + away + 9 - 4 * c) % 8
        before = flag(4 * c + e < turn + 1)
        for k in range(2):
            real = (e < PAIRS) & ((before == 0) | (tile > 0))
            if away == 0:
                real = real & ((before == 1) | (c != k))

            @pl.when(real)
            def _(before=before, at=at, k=k):
                greet((tile - before, 2 * at + k))

        to, real = sum_source(at)

        @pl.when(real)
        def _(to=to):
            greet(to)

    greet((tile, other))

    get_own = pltpu.make_async_copy(ir, ir_v.at[c], ir_own)
    get_own.start()
    get_forward = pltpu.make_async_copy(forward, fwd_v, table_sem.at[0])
    get_forward.start()
    get_inverse = pltpu.make_async_copy(inverse, inv_v, table_sem.at[1])
    get_inverse.start()

    def sample_target(away, d):
        at = (z + away) % 8
        back = at - 4 * (at // 4)
        e = (z + back + 9 - 4 * d) % 8
        ahead = flag(4 * d + e < back + 1)
        there = (e < PAIRS) & ((ahead == 0) | (tile < tiles - 1))
        itself = (away == 0) & (e < PAIRS) & (ahead == 0) & (d == c)
        return at, e, ahead, there, itself

    def sum_target(g, k):
        ahead = upper * c
        at = 4 * (upper + c - 2 * ahead) + g
        there = (ahead == 0) | (tile < tiles - 1)
        itself = (ahead == 0) & (at == z) & (k == c)
        return (tile + ahead, 2 * at + k), there, itself

    _, _, _, _, own_is_in = sample_target(0, c)
    _, _, own_is_out = sum_target(z % 4, c)
    last = flag(tile == tiles - 1)
    awaited = 1 + 2 * PAIRS + CHIPS - flag(own_is_in) - flag(own_is_out)
    awaited = awaited - last * (2 * jnp.maximum(z - 3, 0) + 8 * upper * c)
    get_samples.wait()
    pl.semaphore_wait(barrier, awaited)

    for window in range(2):
        for away in far_first[::-1]:
            d = ((z + away) % 8 // 4 + window) % 2
            at, e, ahead, there, itself = sample_target(away, d)
            if away == 0:

                @pl.when(itself)
                def _(e=e):
                    pltpu.make_async_copy(mine, held.at[e, c], in_recv.at[e, c]).start()

            @pl.when(there & jnp.logical_not(itself))
            def _(at=at, e=e, ahead=ahead, away=away, d=d):
                pltpu.make_async_remote_copy(
                    src_ref=mine,
                    dst_ref=held.at[e, c],
                    send_sem=in_send.at[away, d],
                    recv_sem=in_recv.at[e, c],
                    device_id=(tile + ahead, 2 * at + d),
                    device_id_type=MESH,
                ).start()

    send_ir = pltpu.make_async_remote_copy(
        src_ref=ir,
        dst_ref=ir_v.at[c],
        send_sem=ir_send,
        recv_sem=ir_recv,
        device_id=(tile, other),
        device_id_type=MESH,
    )
    send_ir.start()

    get_lengths.wait()
    get_rooms.wait()
    place = lax.broadcasted_iota(jnp.int32, (8, 128), 0) * 128 + lax.broadcasted_iota(
        jnp.int32, (8, 128), 1
    )
    base = tile * (2 * OUT) + (upper + c) * OUT
    block = base + place // PARTS
    delay = z * PARTS + place % PARTS
    row_block = base - z * PARTS - PARTS + place
    begin = jnp.zeros((8, 128), jnp.int32)
    room = jnp.zeros((8, 128), jnp.int32)
    joined = jnp.ones((8, 128), jnp.float32)
    start = jnp.int32(0)
    for n in range(ROOMS):
        end = start + lengths_s[n]
        member = (block >= start) & (block < end)
        begin = jnp.where(member, start, begin)
        room = jnp.where(member, rooms_s[n], room)
        joined = jnp.where(row_block == start, 0.0, joined)
        start = end
    chosen = jnp.where(block - delay >= begin, room * PARTS + place % PARTS, NONE)
    choice_v[...] = chosen
    first_v[...] = joined
    put_choice = pltpu.make_async_copy(choice_v, choice, small_sem.at[2])
    put_first = pltpu.make_async_copy(first_v, first, small_sem.at[3])
    put_choice.start()
    put_first.start()

    corner = (lax.broadcasted_iota(jnp.int32, (8, 128), 0) == 0) & (
        lax.broadcasted_iota(jnp.int32, (8, 128), 1) == 0
    )
    filters[NONE] = jnp.zeros((3, 8, 128), jnp.float32)

    def unpack(part):
        def step(n, _):
            for p in range(8):
                unpacked[pl.ds(16 * p, 16), :] = ir_v[part, n, p].astype(jnp.float32)
            for p in range(8):
                hre = unpacked[pl.ds(16 * p, 8, stride=2), :]
                him = unpacked[pl.ds(16 * p + 1, 8, stride=2), :]
                at = n * PARTS + part * 8 + p
                filters[at, 0] = hre
                filters[at, 1] = jnp.where(corner, 0.0, him)
                filters[at, 2] = jnp.where(corner, him, hre)
            return 0

        lax.fori_loop(0, ROOMS, step, 0)

    get_own.wait()
    unpack(c)

    put_choice.wait()
    put_first.wait()
    get_forward.wait()
    get_inverse.wait()
    send_ir.wait_recv()
    unpack(1 - c)

    lane = lax.broadcasted_iota(jnp.int32, (8, 128), 1) % 4
    turn_re = jnp.where(lane == 0, 1.0, jnp.where(lane == 2, -1.0, 0.0))
    turn_im = jnp.where(lane == 1, 1.0, jnp.where(lane == 3, -1.0, 0.0))
    sign = 1.0 - 2.0 * (lane % 2).astype(jnp.float32)

    down = ((z + 4 - 2 * (upper + c)) % 4 + 1) // 2 % 2
    down = jnp.maximum(down, flag((z == 0) & (c == 0)))
    late = down * ((upper + c + 1) % 2)
    swap = down - late

    def frame(row, opens, before_re, before_im, own_re, own_im):
        frame_re = opens * before_re + sign * own_re
        frame_im = opens * before_im + sign * own_im
        to = pl.multiple_of(SUB * row, 8)
        spectra[pl.ds(to, 8), :] = frame_re.astype(jnp.bfloat16).astype(jnp.float32)
        spectra[pl.ds(to + 8, 8), :] = frame_im.astype(jnp.bfloat16).astype(jnp.float32)

    def pair(step, _):
        e = step + down * (PAIRS - 1 - 2 * step)

        @pl.when((tile > 0) | (4 * c + e >= turn + 1))
        def _():
            for k in range(2):
                pltpu.make_async_copy(samples, held.at[e, k], in_recv.at[e, k]).wait()

        x = held[e].astype(jnp.float32).reshape(16, W)
        x = jnp.concatenate([x[:, : W // 2], x[:, W // 2 :]], axis=0).astype(jnp.bfloat16)
        for n in range(2 * W // 256):
            g = jnp.dot(x, fwd_v[:, 256 * n : 256 * n + 256], preferred_element_type=jnp.float32)
            raw[pl.ds(2 * n, 32, stride=SUB), :] = g[:, :128]
            raw[pl.ds(2 * n + 1, 32, stride=SUB), :] = g[:, 128:]
        before_re, before_im = None, None
        for r in range(16):
            first_re, first_im = raw[SUB * r : SUB * r + 8, :], raw[SUB * r + 8 : SUB * r + 16, :]
            at = SUB * (16 + r)
            then_re, then_im = raw[at : at + 8, :], raw[at + 8 : at + 16, :]
            own_re = first_re + (turn_re * then_re + turn_im * then_im)
            own_im = first_im + (turn_re * then_im - turn_im * then_re)
            if r == 0:
                edges_v[e, 0, 0] = own_re
                edges_v[e, 0, 1] = own_im
            else:
                frame(16 * e + r, first[0, 16 * e + r], before_re, before_im, own_re, own_im)
            before_re, before_im = own_re, own_im
        edges_v[e, 1, 0] = before_re
        edges_v[e, 1, 1] = before_im

        def half_sums(m, _):
            h32 = m + swap * (1 - 2 * m)
            for n in range(2):
                b = 2 * h32 + n
                row = 16 * b + 16
                tail_re, tail_im = edges_v[b, 1, 0], edges_v[b, 1, 1]
                head_re, head_im = edges_v[b + 1, 0, 0], edges_v[b + 1, 0, 1]
                frame(row, first[0, row], tail_re, tail_im, head_re, head_im)

            def eight(b, _):
                res = [jnp.zeros((8, 128), jnp.float32) for _ in range(8)]
                ims = [jnp.zeros((8, 128), jnp.float32) for _ in range(8)]
                for p in range(PARTS):
                    for t in range(8):
                        at = pl.multiple_of(SUB * (32 * h32 + 8 * b + t - p + PARTS), 8)
                        are = spectra[pl.ds(at, 8), :]
                        aim = spectra[pl.ds(at + 8, 8), :]
                        h = choice[4 * h32 + b, 16 * t + p]
                        h0, h1, h2 = filters[h, 0], filters[h, 1], filters[h, 2]
                        res[t] = res[t] + (are * h0 - aim * h1)
                        ims[t] = ims[t] + (are * h1 + aim * h2)
                for t in range(8):
                    to = pl.multiple_of(SUB * (8 * b + t), 8)
                    summed[pl.ds(to, 8), :] = res[t]
                    summed[pl.ds(to + 8, 8), :] = ims[t]
                    summed[pl.ds(32 * SUB + to, 8), :] = turn_re * res[t] - turn_im * ims[t]
                    summed[pl.ds(32 * SUB + to + 8, 8), :] = turn_re * ims[t] + turn_im * res[t]
                return 0

            lax.fori_loop(0, 4, eight, 0)

            y = jnp.concatenate(
                [summed[pl.ds(j, 64, stride=SUB), :].astype(jnp.bfloat16) for j in range(SUB)],
                axis=1,
            )
            for n in range(W // 512):
                v = jnp.dot(
                    y, inv_v[:, 256 * n : 256 * n + 256], preferred_element_type=jnp.float32
                )
                for q in range(8):
                    left = 512 * (q // 4) + 256 * n
                    parts_out[4 * h32 + q % 4, :, left : left + 256] = v[8 * q : 8 * q + 8].astype(
                        jnp.bfloat16
                    )
            for in_half in range(2):
                g = 2 * h32 + in_half
                for k in range(2):
                    to, there, itself = sum_target(g, k)

                    @pl.when(itself)
                    def _(k=k, g=g):
                        pltpu.make_async_copy(
                            parts_out.at[2 * g + k], arrived.at[z], out_recv.at[z]
                        ).start()

                    @pl.when(there & jnp.logical_not(itself))
                    def _(k=k, g=g, to=to):
                        pltpu.make_async_remote_copy(
                            src_ref=parts_out.at[2 * g + k],
                            dst_ref=arrived.at[z],
                            send_sem=out_send.at[2 * g + k],
                            recv_sem=out_recv.at[z],
                            device_id=to,
                            device_id_type=MESH,
                        ).start()

            return 0

        at_third, at_last = flag(step == 2), flag(step == 4)
        begun = at_last * (1 - late)
        lax.fori_loop(begun, at_third * (1 - late) + 2 * at_last, half_sums, 0)
        return 0

    lax.fori_loop(0, PAIRS, pair, 0)

    send_ir.wait_send()
    for away in range(CHIPS):
        for d in range(2):
            _, _, _, there, itself = sample_target(away, d)

            @pl.when(there & jnp.logical_not(itself))
            def _(away=away, d=d):
                pltpu.make_async_copy(samples, held.at[0, 0], in_send.at[away, d]).wait()

    for g in range(4):
        for k in range(2):
            _, there, itself = sum_target(g, k)

            @pl.when(there & jnp.logical_not(itself))
            def _(g=g, k=k):
                pltpu.make_async_copy(
                    parts_out.at[2 * g + k], arrived.at[0], out_send.at[2 * g + k]
                ).wait()

    total = jnp.zeros((ROWS, W), jnp.float32)
    for zs in range(CHIPS):

        @pl.when((tile > 0) | (upper == 1) | (zs < 4))
        def _(zs=zs):
            pltpu.make_async_copy(parts_out.at[0], arrived.at[zs], out_recv.at[zs]).wait()

        total = total + arrived[zs].astype(jnp.float32)
    out[...] = total


def on_device(samples, ir_spectra, clip_lengths, room_ids):
    rooms, parts = ir_spectra.shape[0], ir_spectra.shape[1]
    ir = ir_spectra.reshape(rooms, parts, 2, W // 128, 128)
    ir = ir.transpose(0, 1, 3, 2, 4).reshape(rooms, parts, SUB, 128)
    hbm = pl.BlockSpec(memory_space=pltpu.HBM)
    bf16, f32, dma = jnp.bfloat16, jnp.float32, pltpu.SemaphoreType.DMA
    return pl.pallas_call(
        kernel,
        out_shape=jax.ShapeDtypeStruct((ROWS, W), f32),
        in_specs=[hbm] * 6,
        out_specs=pl.BlockSpec(memory_space=pltpu.VMEM),
        scratch_shapes=[
            pltpu.VMEM((W // 2, 2 * W), bf16),
            pltpu.VMEM((2 * W, W // 2), bf16),
            pltpu.VMEM((2, ROOMS, 8, SUB, 128), bf16),
            pltpu.VMEM((NONE + 1, 3, 8, 128), f32),
            pltpu.VMEM((128, 128), f32),
            pltpu.VMEM((ROWS, W), bf16),
            pltpu.VMEM((PAIRS, 2, ROWS, W), bf16),
            pltpu.VMEM((32 * SUB, 128), f32),
            pltpu.VMEM((SPAN * SUB, 128), f32),
            pltpu.VMEM((PAIRS, 2, 2, 8, 128), f32),
            pltpu.VMEM((64 * SUB, 128), f32),
            pltpu.VMEM((8, ROWS, W), bf16),
            pltpu.VMEM((CHIPS, ROWS, W), bf16),
            pltpu.VMEM((8, 128), jnp.int32),
            pltpu.VMEM((8, 128), f32),
            pltpu.SMEM((8, 128), jnp.int32),
            pltpu.SMEM((8, 128), f32),
            pltpu.SMEM((ROOMS,), jnp.int32),
            pltpu.SMEM((ROOMS,), jnp.int32),
            dma((4,)),
            dma((2,)),
            dma,
            dma,
            dma,
            dma((CHIPS, 2)),
            dma((PAIRS, 2)),
            dma((8,)),
            dma((CHIPS,)),
        ],
        compiler_params=pltpu.CompilerParams(
            collective_id=0, has_side_effects=True, vmem_limit_bytes=48 * 1024 * 1024
        ),
    )(
        *[
            pltpu.with_memory_space_constraint(x, pltpu.HBM)
            for x in (samples, ir, clip_lengths, room_ids, forward_part(W), inverse_part(W))
        ]
    )


def solution(mesh):
    in_specs = (P(("tile", "ir"), None), P(None, "ir", None, None), P(), P())
    out_specs = P(("tile", "ir"), None)
    return jax.shard_map(
        on_device, mesh=mesh, in_specs=in_specs, out_specs=out_specs, check_vma=False
    )
```

```python
import jax
import jax.numpy as jnp
import numpy as np
from jax import lax
from jax.experimental import pallas as pl
from jax.experimental.pallas import tpu as pltpu
from jax.sharding import PartitionSpec as P

MESH = pl.DeviceIdType.MESH
W = 1024
ROWS = 8
CHIPS = 8
ROOMS = 16
PARTS = 16
OUT = 64
PAIRS = 5
SPAN = PAIRS * 2 * ROWS
SUB = 2 * W // 128
NONE = ROOMS * PARTS


def forward_part(width):
    length = 2 * width
    sample = np.arange(width // 2)
    bins = np.arange(width)
    phase = sample[:, None] * bins[None, :] % length
    angle = phase * (2.0 * np.pi / length)
    parity = np.where(sample % 2 == 0, 1.0, -1.0)
    sines = np.where(bins[None, :] == 0, parity[:, None], -np.sin(angle))
    table = np.concatenate([np.cos(angle), sines], axis=1)
    return jnp.asarray(table, dtype=jnp.float32).astype(jnp.bfloat16)


def inverse_part(width):
    length = 2 * width
    bins = np.arange(width)
    outputs = width + np.arange(width // 2)
    phase = bins[:, None] * outputs[None, :] % length
    angle = phase * (2.0 * np.pi / length)
    weight = np.where(bins == 0, 1.0, 2.0)[:, None] / length
    parity = np.where(outputs % 2 == 0, 1.0, -1.0)[None, :] / length
    cosines = weight * np.cos(angle)
    sines = np.where(bins[:, None] == 0, parity, -weight * np.sin(angle))
    table = np.concatenate([cosines, sines], axis=0)
    return jnp.asarray(table, dtype=jnp.float32).astype(jnp.bfloat16)


def kernel(
    samples,
    ir,
    lengths,
    rooms,
    forward,
    inverse,
    out,
    fwd_v,
    inv_v,
    ir_v,
    filters,
    unpacked,
    mine,
    held,
    raw,
    spectra,
    edges_v,
    summed,
    parts_out,
    arrived,
    choice_v,
    first_v,
    choice,
    first,
    lengths_s,
    rooms_s,
    small_sem,
    table_sem,
    ir_send,
    ir_recv,
    ir_own,
    in_send,
    in_recv,
    out_send,
    out_recv,
):
    tile, ir_at = lax.axis_index("tile"), lax.axis_index("ir")
    tiles = lax.axis_size("tile")
    z, c = ir_at // 2, ir_at % 2
    upper = z // 4
    turn = z - 4 * upper
    other = 2 * z + 1 - c
    far_first = (4, 3, 5, 2, 6, 1, 7, 0)

    get_lengths = pltpu.make_async_copy(lengths, lengths_s, small_sem.at[0])
    get_rooms = pltpu.make_async_copy(rooms, rooms_s, small_sem.at[1])
    get_samples = pltpu.make_async_copy(samples, mine, small_sem.at[3])

    @pl.when(tile == 0)
    def _():
        held[...] = jnp.zeros(held.shape, held.dtype)
        arrived[...] = jnp.zeros(arrived.shape, arrived.dtype)

    barrier = pltpu.get_barrier_semaphore()

    def flag(x):
        return x.astype(jnp.int32)

    def greet(to):
        pl.semaphore_signal(barrier, inc=1, device_id=to, device_id_type=MESH)

    def sum_source(at):
        from_upper = at // 4
        before = from_upper * (1 - upper)
        core = upper + from_upper * (1 - 2 * upper)
        real = ((before == 0) | (tile > 0)) & ((at != z) | (before == 1) | (core != c))
        return (tile - before, 2 * at + core), real

    for away in far_first:
        at = (z + away) % 8
        e = (z + turn + away + 9 - 4 * c) % 8
        before = flag(4 * c + e < turn + 1)
        for k in range(2):
            real = (e < PAIRS) & ((before == 0) | (tile > 0))
            if away == 0:
                real = real & ((before == 1) | (c != k))

            @pl.when(real)
            def _(before=before, at=at, k=k):
                greet((tile - before, 2 * at + k))

        to, real = sum_source(at)

        @pl.when(real)
        def _(to=to):
            greet(to)

    greet((tile, other))
    get_samples.start()
    get_lengths.start()
    get_rooms.start()

    get_own = pltpu.make_async_copy(ir, ir_v.at[c], ir_own)
    get_own.start()
    get_forward = pltpu.make_async_copy(forward, fwd_v, table_sem.at[0])
    get_forward.start()
    get_inverse = pltpu.make_async_copy(inverse, inv_v, table_sem.at[1])
    get_inverse.start()

    def sample_target(away, d):
        at = (z + away) % 8
        back = at - 4 * (at // 4)
        e = (z + back + 9 - 4 * d) % 8
        ahead = flag(4 * d + e < back + 1)
        there = (e < PAIRS) & ((ahead == 0) | (tile < tiles - 1))
        itself = (away == 0) & (e < PAIRS) & (ahead == 0) & (d == c)
        return at, e, ahead, there, itself

    def sum_target(g, k):
        ahead = upper * c
        at = 4 * (upper + c - 2 * ahead) + g
        there = (ahead == 0) | (tile < tiles - 1)
        itself = (ahead == 0) & (at == z) & (k == c)
        return (tile + ahead, 2 * at + k), there, itself

    _, _, _, _, own_is_in = sample_target(0, c)
    _, _, own_is_out = sum_target(z % 4, c)
    last = flag(tile == tiles - 1)
    awaited = 1 + 2 * PAIRS + CHIPS - flag(own_is_in) - flag(own_is_out)
    awaited = awaited - last * (2 * jnp.maximum(z - 3, 0) + 8 * upper * c)
    get_samples.wait()
    pl.semaphore_wait(barrier, awaited)

    for window in range(2):
        for away in (1, 2, 3, 4, 7, 6, 5, 0):
            d = ((z + away) % 8 // 4 + window) % 2
            at, e, ahead, there, itself = sample_target(away, d)
            if away == 0:

                @pl.when(itself)
                def _(e=e):
                    pltpu.make_async_copy(mine, held.at[e, c], in_recv.at[e, c]).start()

            @pl.when(there & jnp.logical_not(itself))
            def _(at=at, e=e, ahead=ahead, away=away, d=d):
                pltpu.make_async_remote_copy(
                    src_ref=mine,
                    dst_ref=held.at[e, c],
                    send_sem=in_send.at[away, d],
                    recv_sem=in_recv.at[e, c],
                    device_id=(tile + ahead, 2 * at + d),
                    device_id_type=MESH,
                ).start()

    send_ir = pltpu.make_async_remote_copy(
        src_ref=ir,
        dst_ref=ir_v.at[c],
        send_sem=ir_send,
        recv_sem=ir_recv,
        device_id=(tile, other),
        device_id_type=MESH,
    )
    send_ir.start()

    get_lengths.wait()
    get_rooms.wait()
    place = lax.broadcasted_iota(jnp.int32, (8, 128), 0) * 128 + lax.broadcasted_iota(
        jnp.int32, (8, 128), 1
    )
    base = tile * (2 * OUT) + (upper + c) * OUT
    block = base + place // PARTS
    delay = z * PARTS + place % PARTS
    row_block = base - z * PARTS - PARTS + place
    begin = jnp.zeros((8, 128), jnp.int32)
    room = jnp.zeros((8, 128), jnp.int32)
    joined = jnp.ones((8, 128), jnp.float32)
    start = jnp.int32(0)
    for n in range(ROOMS):
        end = start + lengths_s[n]
        member = (block >= start) & (block < end)
        begin = jnp.where(member, start, begin)
        room = jnp.where(member, rooms_s[n], room)
        joined = jnp.where(row_block == start, 0.0, joined)
        start = end
    chosen = jnp.where(block - delay >= begin, room * PARTS + place % PARTS, NONE)
    choice_v[...] = chosen
    first_v[...] = joined
    put_choice = pltpu.make_async_copy(choice_v, choice, small_sem.at[2])
    put_first = pltpu.make_async_copy(first_v, first, small_sem.at[3])
    put_choice.start()
    put_first.start()

    corner = (lax.broadcasted_iota(jnp.int32, (8, 128), 0) == 0) & (
        lax.broadcasted_iota(jnp.int32, (8, 128), 1) == 0
    )
    filters[NONE] = jnp.zeros((3, 8, 128), jnp.float32)

    def unpack(part):
        def step(n, _):
            for p in range(8):
                unpacked[pl.ds(16 * p, 16), :] = ir_v[part, n, p].astype(jnp.float32)
            for p in range(8):
                hre = unpacked[pl.ds(16 * p, 8, stride=2), :]
                him = unpacked[pl.ds(16 * p + 1, 8, stride=2), :]
                at = n * PARTS + part * 8 + p
                filters[at, 0] = hre
                filters[at, 1] = jnp.where(corner, 0.0, him)
                filters[at, 2] = jnp.where(corner, him, hre)
            return 0

        lax.fori_loop(0, ROOMS, step, 0)

    get_own.wait()
    unpack(c)

    put_choice.wait()
    put_first.wait()
    get_forward.wait()
    get_inverse.wait()
    send_ir.wait_recv()
    unpack(1 - c)

    lane = lax.broadcasted_iota(jnp.int32, (8, 128), 1) % 4
    turn_re = jnp.where(lane == 0, 1.0, jnp.where(lane == 2, -1.0, 0.0))
    turn_im = jnp.where(lane == 1, 1.0, jnp.where(lane == 3, -1.0, 0.0))
    sign = 1.0 - 2.0 * (lane % 2).astype(jnp.float32)

    down = ((z + 4 - 2 * (upper + c)) % 4 + 1) // 2 % 2
    down = jnp.maximum(down, flag((z == 0) & (c == 0)))
    late = down * ((upper + c + 1) % 2)
    swap = down - late

    def frame(row, opens, before_re, before_im, own_re, own_im):
        frame_re = opens * before_re + sign * own_re
        frame_im = opens * before_im + sign * own_im
        to = pl.multiple_of(SUB * row, 8)
        spectra[pl.ds(to, 8), :] = frame_re.astype(jnp.bfloat16).astype(jnp.float32)
        spectra[pl.ds(to + 8, 8), :] = frame_im.astype(jnp.bfloat16).astype(jnp.float32)

    def pair(step, _):
        e = step + down * (PAIRS - 1 - 2 * step)

        @pl.when((tile > 0) | (4 * c + e >= turn + 1))
        def _():
            for k in range(2):
                pltpu.make_async_copy(samples, held.at[e, k], in_recv.at[e, k]).wait()

        x = held[e].astype(jnp.float32).reshape(16, W)
        x = jnp.concatenate([x[:, : W // 2], x[:, W // 2 :]], axis=0).astype(jnp.bfloat16)
        for n in range(2 * W // 256):
            g = jnp.dot(x, fwd_v[:, 256 * n : 256 * n + 256], preferred_element_type=jnp.float32)
            raw[pl.ds(2 * n, 32, stride=SUB), :] = g[:, :128]
            raw[pl.ds(2 * n + 1, 32, stride=SUB), :] = g[:, 128:]
        before_re, before_im = None, None
        for r in range(16):
            first_re, first_im = raw[SUB * r : SUB * r + 8, :], raw[SUB * r + 8 : SUB * r + 16, :]
            at = SUB * (16 + r)
            then_re, then_im = raw[at : at + 8, :], raw[at + 8 : at + 16, :]
            own_re = first_re + (turn_re * then_re + turn_im * then_im)
            own_im = first_im + (turn_re * then_im - turn_im * then_re)
            if r == 0:
                edges_v[e, 0, 0] = own_re
                edges_v[e, 0, 1] = own_im
            else:
                frame(16 * e + r, first[0, 16 * e + r], before_re, before_im, own_re, own_im)
            before_re, before_im = own_re, own_im
        edges_v[e, 1, 0] = before_re
        edges_v[e, 1, 1] = before_im

        def half_sums(m, _):
            h32 = m + swap * (1 - 2 * m)
            for n in range(2):
                b = 2 * h32 + n
                row = 16 * b + 16
                tail_re, tail_im = edges_v[b, 1, 0], edges_v[b, 1, 1]
                head_re, head_im = edges_v[b + 1, 0, 0], edges_v[b + 1, 0, 1]
                frame(row, first[0, row], tail_re, tail_im, head_re, head_im)

            def eight(b, _):
                res = [jnp.zeros((8, 128), jnp.float32) for _ in range(8)]
                ims = [jnp.zeros((8, 128), jnp.float32) for _ in range(8)]
                for p in range(PARTS):
                    for t in range(8):
                        at = pl.multiple_of(SUB * (32 * h32 + 8 * b + t - p + PARTS), 8)
                        are = spectra[pl.ds(at, 8), :]
                        aim = spectra[pl.ds(at + 8, 8), :]
                        h = choice[4 * h32 + b, 16 * t + p]
                        h0, h1, h2 = filters[h, 0], filters[h, 1], filters[h, 2]
                        res[t] = res[t] + (are * h0 - aim * h1)
                        ims[t] = ims[t] + (are * h1 + aim * h2)
                for t in range(8):
                    to = pl.multiple_of(SUB * (8 * b + t), 8)
                    summed[pl.ds(to, 8), :] = res[t]
                    summed[pl.ds(to + 8, 8), :] = ims[t]
                    summed[pl.ds(32 * SUB + to, 8), :] = turn_re * res[t] - turn_im * ims[t]
                    summed[pl.ds(32 * SUB + to + 8, 8), :] = turn_re * ims[t] + turn_im * res[t]
                return 0

            lax.fori_loop(0, 4, eight, 0)

            y = jnp.concatenate(
                [summed[pl.ds(j, 64, stride=SUB), :].astype(jnp.bfloat16) for j in range(SUB)],
                axis=1,
            )
            for n in range(W // 512):
                v = jnp.dot(
                    y, inv_v[:, 256 * n : 256 * n + 256], preferred_element_type=jnp.float32
                )
                for q in range(8):
                    left = 512 * (q // 4) + 256 * n
                    parts_out[4 * h32 + q % 4, :, left : left + 256] = v[8 * q : 8 * q + 8].astype(
                        jnp.bfloat16
                    )
            for in_half in range(2):
                g = 2 * h32 + in_half
                for k in range(2):
                    to, there, itself = sum_target(g, k)

                    @pl.when(itself)
                    def _(k=k, g=g):
                        pltpu.make_async_copy(
                            parts_out.at[2 * g + k], arrived.at[z], out_recv.at[z]
                        ).start()

                    @pl.when(there & jnp.logical_not(itself))
                    def _(k=k, g=g, to=to):
                        pltpu.make_async_remote_copy(
                            src_ref=parts_out.at[2 * g + k],
                            dst_ref=arrived.at[z],
                            send_sem=out_send.at[2 * g + k],
                            recv_sem=out_recv.at[z],
                            device_id=to,
                            device_id_type=MESH,
                        ).start()

            return 0

        at_third, at_last = flag(step == 2), flag(step == 4)
        begun = at_last * (1 - late)
        lax.fori_loop(begun, at_third * (1 - late) + 2 * at_last, half_sums, 0)
        return 0

    lax.fori_loop(0, PAIRS, pair, 0)

    send_ir.wait_send()
    for away in range(CHIPS):
        for d in range(2):
            _, _, _, there, itself = sample_target(away, d)

            @pl.when(there & jnp.logical_not(itself))
            def _(away=away, d=d):
                pltpu.make_async_copy(samples, held.at[0, 0], in_send.at[away, d]).wait()

    for g in range(4):
        for k in range(2):
            _, there, itself = sum_target(g, k)

            @pl.when(there & jnp.logical_not(itself))
            def _(g=g, k=k):
                pltpu.make_async_copy(
                    parts_out.at[2 * g + k], arrived.at[0], out_send.at[2 * g + k]
                ).wait()

    total = jnp.zeros((ROWS, W), jnp.float32)
    for zs in range(CHIPS):

        @pl.when((tile > 0) | (upper == 1) | (zs < 4))
        def _(zs=zs):
            pltpu.make_async_copy(parts_out.at[0], arrived.at[zs], out_recv.at[zs]).wait()

        total = total + arrived[zs].astype(jnp.float32)
    out[...] = total


def on_device(samples, ir_spectra, clip_lengths, room_ids):
    rooms, parts = ir_spectra.shape[0], ir_spectra.shape[1]
    ir = ir_spectra.reshape(rooms, parts, 2, W // 128, 128)
    ir = ir.transpose(0, 1, 3, 2, 4).reshape(rooms, parts, SUB, 128)
    hbm = pl.BlockSpec(memory_space=pltpu.HBM)
    bf16, f32, dma = jnp.bfloat16, jnp.float32, pltpu.SemaphoreType.DMA
    return pl.pallas_call(
        kernel,
        out_shape=jax.ShapeDtypeStruct((ROWS, W), f32),
        in_specs=[hbm] * 6,
        out_specs=pl.BlockSpec(memory_space=pltpu.VMEM),
        scratch_shapes=[
            pltpu.VMEM((W // 2, 2 * W), bf16),
            pltpu.VMEM((2 * W, W // 2), bf16),
            pltpu.VMEM((2, ROOMS, 8, SUB, 128), bf16),
            pltpu.VMEM((NONE + 1, 3, 8, 128), f32),
            pltpu.VMEM((128, 128), f32),
            pltpu.VMEM((ROWS, W), bf16),
            pltpu.VMEM((PAIRS, 2, ROWS, W), bf16),
            pltpu.VMEM((32 * SUB, 128), f32),
            pltpu.VMEM((SPAN * SUB, 128), f32),
            pltpu.VMEM((PAIRS, 2, 2, 8, 128), f32),
            pltpu.VMEM((64 * SUB, 128), f32),
            pltpu.VMEM((8, ROWS, W), bf16),
            pltpu.VMEM((CHIPS, ROWS, W), bf16),
            pltpu.VMEM((8, 128), jnp.int32),
            pltpu.VMEM((8, 128), f32),
            pltpu.SMEM((8, 128), jnp.int32),
            pltpu.SMEM((8, 128), f32),
            pltpu.SMEM((ROOMS,), jnp.int32),
            pltpu.SMEM((ROOMS,), jnp.int32),
            dma((4,)),
            dma((2,)),
            dma,
            dma,
            dma,
            dma((CHIPS, 2)),
            dma((PAIRS, 2)),
            dma((8,)),
            dma((CHIPS,)),
        ],
        compiler_params=pltpu.CompilerParams(
            collective_id=0, has_side_effects=True, vmem_limit_bytes=48 * 1024 * 1024
        ),
    )(
        *[
            pltpu.with_memory_space_constraint(x, pltpu.HBM)
            for x in (samples, ir, clip_lengths, room_ids, forward_part(W), inverse_part(W))
        ]
    )


def solution(mesh):
    in_specs = (P(("tile", "ir"), None), P(None, "ir", None, None), P(), P())
    out_specs = P(("tile", "ir"), None)
    return jax.shard_map(
        on_device, mesh=mesh, in_specs=in_specs, out_specs=out_specs, check_vma=False
    )
```

```python
import jax
import jax.numpy as jnp
import numpy as np
from jax import lax
from jax.experimental import pallas as pl
from jax.experimental.pallas import tpu as pltpu
from jax.sharding import PartitionSpec as P

MESH = pl.DeviceIdType.MESH
W = 1024
ROWS = 8
CHIPS = 8
ROOMS = 16
PARTS = 16
OUT = 64
PAIRS = 5
SPAN = PAIRS * 2 * ROWS
SUB = 2 * W // 128
NONE = ROOMS * PARTS


def forward_part(width):
    length = 2 * width
    sample = np.arange(width // 2)
    bins = np.arange(width)
    phase = sample[:, None] * bins[None, :] % length
    angle = phase * (2.0 * np.pi / length)
    parity = np.where(sample % 2 == 0, 1.0, -1.0)
    sines = np.where(bins[None, :] == 0, parity[:, None], -np.sin(angle))
    table = np.concatenate([np.cos(angle), sines], axis=1)
    return jnp.asarray(table, dtype=jnp.float32).astype(jnp.bfloat16)


def inverse_part(width):
    length = 2 * width
    bins = np.arange(width)
    outputs = width + np.arange(width // 2)
    phase = bins[:, None] * outputs[None, :] % length
    angle = phase * (2.0 * np.pi / length)
    weight = np.where(bins == 0, 1.0, 2.0)[:, None] / length
    parity = np.where(outputs % 2 == 0, 1.0, -1.0)[None, :] / length
    cosines = weight * np.cos(angle)
    sines = np.where(bins[:, None] == 0, parity, -weight * np.sin(angle))
    table = np.concatenate([cosines, sines], axis=0)
    return jnp.asarray(table, dtype=jnp.float32).astype(jnp.bfloat16)


def kernel(
    samples,
    ir,
    lengths,
    rooms,
    forward,
    inverse,
    out,
    fwd_v,
    inv_v,
    ir_v,
    filters,
    unpacked,
    mine,
    held,
    raw,
    spectra,
    edges_v,
    summed,
    parts_out,
    arrived,
    choice_v,
    first_v,
    choice,
    first,
    lengths_s,
    rooms_s,
    small_sem,
    table_sem,
    ir_send,
    ir_recv,
    ir_own,
    in_send,
    in_recv,
    out_send,
    out_recv,
):
    tile, ir_at = lax.axis_index("tile"), lax.axis_index("ir")
    tiles = lax.axis_size("tile")
    z, c = ir_at // 2, ir_at % 2
    upper = z // 4
    turn = z - 4 * upper
    other = 2 * z + 1 - c
    far_first = (4, 3, 5, 2, 6, 1, 7, 0)

    get_lengths = pltpu.make_async_copy(lengths, lengths_s, small_sem.at[0])
    get_rooms = pltpu.make_async_copy(rooms, rooms_s, small_sem.at[1])
    get_samples = pltpu.make_async_copy(samples, mine, small_sem.at[3])

    @pl.when(tile == 0)
    def _():
        held[...] = jnp.zeros(held.shape, held.dtype)
        arrived[...] = jnp.zeros(arrived.shape, arrived.dtype)

    barrier = pltpu.get_barrier_semaphore()

    def flag(x):
        return x.astype(jnp.int32)

    def greet(to):
        pl.semaphore_signal(barrier, inc=1, device_id=to, device_id_type=MESH)

    def sum_source(at):
        from_upper = at // 4
        before = from_upper * (1 - upper)
        core = upper + from_upper * (1 - 2 * upper)
        real = ((before == 0) | (tile > 0)) & ((at != z) | (before == 1) | (core != c))
        return (tile - before, 2 * at + core), real

    for away in far_first:
        at = (z + away) % 8
        e = (z + turn + away + 9 - 4 * c) % 8
        before = flag(4 * c + e < turn + 1)
        for k in range(2):
            real = (e < PAIRS) & ((before == 0) | (tile > 0))
            if away == 0:
                real = real & ((before == 1) | (c != k))

            @pl.when(real)
            def _(before=before, at=at, k=k):
                greet((tile - before, 2 * at + k))

        to, real = sum_source(at)

        @pl.when(real)
        def _(to=to):
            greet(to)

    greet((tile, other))
    get_samples.start()
    get_lengths.start()
    get_rooms.start()

    get_own = pltpu.make_async_copy(ir, ir_v.at[c], ir_own)
    get_own.start()
    get_forward = pltpu.make_async_copy(forward, fwd_v, table_sem.at[0])
    get_forward.start()
    get_inverse = pltpu.make_async_copy(inverse, inv_v, table_sem.at[1])
    get_inverse.start()

    def sample_target(away, d):
        at = (z + away) % 8
        back = at - 4 * (at // 4)
        e = (z + back + 9 - 4 * d) % 8
        ahead = flag(4 * d + e < back + 1)
        there = (e < PAIRS) & ((ahead == 0) | (tile < tiles - 1))
        itself = (away == 0) & (e < PAIRS) & (ahead == 0) & (d == c)
        return at, e, ahead, there, itself

    def sum_target(g, k):
        ahead = upper * c
        at = 4 * (upper + c - 2 * ahead) + g
        there = (ahead == 0) | (tile < tiles - 1)
        itself = (ahead == 0) & (at == z) & (k == c)
        return (tile + ahead, 2 * at + k), there, itself

    _, _, _, _, own_is_in = sample_target(0, c)
    _, _, own_is_out = sum_target(z % 4, c)
    last = flag(tile == tiles - 1)
    awaited = 1 + 2 * PAIRS + CHIPS - flag(own_is_in) - flag(own_is_out)
    awaited = awaited - last * (2 * jnp.maximum(z - 3, 0) + 8 * upper * c)
    get_samples.wait()
    pl.semaphore_wait(barrier, awaited)

    send_ir = pltpu.make_async_remote_copy(
        src_ref=ir,
        dst_ref=ir_v.at[c],
        send_sem=ir_send,
        recv_sem=ir_recv,
        device_id=(tile, other),
        device_id_type=MESH,
    )
    for window in range(2):
        if window == 1:
            send_ir.start()
        for away in (1, 2, 3, 4, 7, 6, 5, 0):
            d = ((z + away) % 8 // 4 + window) % 2
            at, e, ahead, there, itself = sample_target(away, d)
            if away == 0:

                @pl.when(itself)
                def _(e=e):
                    pltpu.make_async_copy(mine, held.at[e, c], in_recv.at[e, c]).start()

            @pl.when(there & jnp.logical_not(itself))
            def _(at=at, e=e, ahead=ahead, away=away, d=d):
                pltpu.make_async_remote_copy(
                    src_ref=mine,
                    dst_ref=held.at[e, c],
                    send_sem=in_send.at[away, d],
                    recv_sem=in_recv.at[e, c],
                    device_id=(tile + ahead, 2 * at + d),
                    device_id_type=MESH,
                ).start()


    get_lengths.wait()
    get_rooms.wait()
    place = lax.broadcasted_iota(jnp.int32, (8, 128), 0) * 128 + lax.broadcasted_iota(
        jnp.int32, (8, 128), 1
    )
    base = tile * (2 * OUT) + (upper + c) * OUT
    block = base + place // PARTS
    delay = z * PARTS + place % PARTS
    row_block = base - z * PARTS - PARTS + place
    begin = jnp.zeros((8, 128), jnp.int32)
    room = jnp.zeros((8, 128), jnp.int32)
    joined = jnp.ones((8, 128), jnp.float32)
    start = jnp.int32(0)
    for n in range(ROOMS):
        end = start + lengths_s[n]
        member = (block >= start) & (block < end)
        begin = jnp.where(member, start, begin)
        room = jnp.where(member, rooms_s[n], room)
        joined = jnp.where(row_block == start, 0.0, joined)
        start = end
    chosen = jnp.where(block - delay >= begin, room * PARTS + place % PARTS, NONE)
    choice_v[...] = chosen
    first_v[...] = joined
    put_choice = pltpu.make_async_copy(choice_v, choice, small_sem.at[2])
    put_first = pltpu.make_async_copy(first_v, first, small_sem.at[3])
    put_choice.start()
    put_first.start()

    corner = (lax.broadcasted_iota(jnp.int32, (8, 128), 0) == 0) & (
        lax.broadcasted_iota(jnp.int32, (8, 128), 1) == 0
    )
    filters[NONE] = jnp.zeros((3, 8, 128), jnp.float32)

    def unpack(part):
        def step(n, _):
            for p in range(8):
                unpacked[pl.ds(16 * p, 16), :] = ir_v[part, n, p].astype(jnp.float32)
            for p in range(8):
                hre = unpacked[pl.ds(16 * p, 8, stride=2), :]
                him = unpacked[pl.ds(16 * p + 1, 8, stride=2), :]
                at = n * PARTS + part * 8 + p
                filters[at, 0] = hre
                filters[at, 1] = jnp.where(corner, 0.0, him)
                filters[at, 2] = jnp.where(corner, him, hre)
            return 0

        lax.fori_loop(0, ROOMS, step, 0)

    get_own.wait()
    unpack(c)

    put_choice.wait()
    put_first.wait()
    get_forward.wait()
    get_inverse.wait()
    send_ir.wait_recv()
    unpack(1 - c)

    lane = lax.broadcasted_iota(jnp.int32, (8, 128), 1) % 4
    turn_re = jnp.where(lane == 0, 1.0, jnp.where(lane == 2, -1.0, 0.0))
    turn_im = jnp.where(lane == 1, 1.0, jnp.where(lane == 3, -1.0, 0.0))
    sign = 1.0 - 2.0 * (lane % 2).astype(jnp.float32)

    down = ((z + 4 - 2 * (upper + c)) % 4 + 1) // 2 % 2
    down = jnp.maximum(down, flag((z == 0) & (c == 0)))
    late = down * ((upper + c + 1) % 2)
    swap = down - late

    def frame(row, opens, before_re, before_im, own_re, own_im):
        frame_re = opens * before_re + sign * own_re
        frame_im = opens * before_im + sign * own_im
        to = pl.multiple_of(SUB * row, 8)
        spectra[pl.ds(to, 8), :] = frame_re.astype(jnp.bfloat16).astype(jnp.float32)
        spectra[pl.ds(to + 8, 8), :] = frame_im.astype(jnp.bfloat16).astype(jnp.float32)

    def pair(step, _):
        e = step + down * (PAIRS - 1 - 2 * step)

        @pl.when((tile > 0) | (4 * c + e >= turn + 1))
        def _():
            for k in range(2):
                pltpu.make_async_copy(samples, held.at[e, k], in_recv.at[e, k]).wait()

        x = held[e].astype(jnp.float32).reshape(16, W)
        x = jnp.concatenate([x[:, : W // 2], x[:, W // 2 :]], axis=0).astype(jnp.bfloat16)
        for n in range(2 * W // 256):
            g = jnp.dot(x, fwd_v[:, 256 * n : 256 * n + 256], preferred_element_type=jnp.float32)
            raw[pl.ds(2 * n, 32, stride=SUB), :] = g[:, :128]
            raw[pl.ds(2 * n + 1, 32, stride=SUB), :] = g[:, 128:]
        before_re, before_im = None, None
        for r in range(16):
            first_re, first_im = raw[SUB * r : SUB * r + 8, :], raw[SUB * r + 8 : SUB * r + 16, :]
            at = SUB * (16 + r)
            then_re, then_im = raw[at : at + 8, :], raw[at + 8 : at + 16, :]
            own_re = first_re + (turn_re * then_re + turn_im * then_im)
            own_im = first_im + (turn_re * then_im - turn_im * then_re)
            if r == 0:
                edges_v[e, 0, 0] = own_re
                edges_v[e, 0, 1] = own_im
            else:
                frame(16 * e + r, first[0, 16 * e + r], before_re, before_im, own_re, own_im)
            before_re, before_im = own_re, own_im
        edges_v[e, 1, 0] = before_re
        edges_v[e, 1, 1] = before_im

        def half_sums(m, _):
            h32 = m + swap * (1 - 2 * m)
            for n in range(2):
                b = 2 * h32 + n
                row = 16 * b + 16
                tail_re, tail_im = edges_v[b, 1, 0], edges_v[b, 1, 1]
                head_re, head_im = edges_v[b + 1, 0, 0], edges_v[b + 1, 0, 1]
                frame(row, first[0, row], tail_re, tail_im, head_re, head_im)

            def eight(b, _):
                res = [jnp.zeros((8, 128), jnp.float32) for _ in range(8)]
                ims = [jnp.zeros((8, 128), jnp.float32) for _ in range(8)]
                for p in range(PARTS):
                    for t in range(8):
                        at = pl.multiple_of(SUB * (32 * h32 + 8 * b + t - p + PARTS), 8)
                        are = spectra[pl.ds(at, 8), :]
                        aim = spectra[pl.ds(at + 8, 8), :]
                        h = choice[4 * h32 + b, 16 * t + p]
                        h0, h1, h2 = filters[h, 0], filters[h, 1], filters[h, 2]
                        res[t] = res[t] + (are * h0 - aim * h1)
                        ims[t] = ims[t] + (are * h1 + aim * h2)
                for t in range(8):
                    to = pl.multiple_of(SUB * (8 * b + t), 8)
                    summed[pl.ds(to, 8), :] = res[t]
                    summed[pl.ds(to + 8, 8), :] = ims[t]
                    summed[pl.ds(32 * SUB + to, 8), :] = turn_re * res[t] - turn_im * ims[t]
                    summed[pl.ds(32 * SUB + to + 8, 8), :] = turn_re * ims[t] + turn_im * res[t]
                return 0

            lax.fori_loop(0, 4, eight, 0)

            y = jnp.concatenate(
                [summed[pl.ds(j, 64, stride=SUB), :].astype(jnp.bfloat16) for j in range(SUB)],
                axis=1,
            )
            for n in range(W // 512):
                v = jnp.dot(
                    y, inv_v[:, 256 * n : 256 * n + 256], preferred_element_type=jnp.float32
                )
                for q in range(8):
                    left = 512 * (q // 4) + 256 * n
                    parts_out[4 * h32 + q % 4, :, left : left + 256] = v[8 * q : 8 * q + 8].astype(
                        jnp.bfloat16
                    )
            for in_half in range(2):
                g = 2 * h32 + in_half
                for k in range(2):
                    to, there, itself = sum_target(g, k)

                    @pl.when(itself)
                    def _(k=k, g=g):
                        pltpu.make_async_copy(
                            parts_out.at[2 * g + k], arrived.at[z], out_recv.at[z]
                        ).start()

                    @pl.when(there & jnp.logical_not(itself))
                    def _(k=k, g=g, to=to):
                        pltpu.make_async_remote_copy(
                            src_ref=parts_out.at[2 * g + k],
                            dst_ref=arrived.at[z],
                            send_sem=out_send.at[2 * g + k],
                            recv_sem=out_recv.at[z],
                            device_id=to,
                            device_id_type=MESH,
                        ).start()

            return 0

        at_third, at_last = flag(step == 2), flag(step == 4)
        begun = at_last * (1 - late)
        lax.fori_loop(begun, at_third * (1 - late) + 2 * at_last, half_sums, 0)
        return 0

    lax.fori_loop(0, PAIRS, pair, 0)

    send_ir.wait_send()
    for away in range(CHIPS):
        for d in range(2):
            _, _, _, there, itself = sample_target(away, d)

            @pl.when(there & jnp.logical_not(itself))
            def _(away=away, d=d):
                pltpu.make_async_copy(samples, held.at[0, 0], in_send.at[away, d]).wait()

    for g in range(4):
        for k in range(2):
            _, there, itself = sum_target(g, k)

            @pl.when(there & jnp.logical_not(itself))
            def _(g=g, k=k):
                pltpu.make_async_copy(
                    parts_out.at[2 * g + k], arrived.at[0], out_send.at[2 * g + k]
                ).wait()

    total = jnp.zeros((ROWS, W), jnp.float32)
    for zs in range(CHIPS):

        @pl.when((tile > 0) | (upper == 1) | (zs < 4))
        def _(zs=zs):
            pltpu.make_async_copy(parts_out.at[0], arrived.at[zs], out_recv.at[zs]).wait()

        total = total + arrived[zs].astype(jnp.float32)
    out[...] = total


def on_device(samples, ir_spectra, clip_lengths, room_ids):
    rooms, parts = ir_spectra.shape[0], ir_spectra.shape[1]
    ir = ir_spectra.reshape(rooms, parts, 2, W // 128, 128)
    ir = ir.transpose(0, 1, 3, 2, 4).reshape(rooms, parts, SUB, 128)
    hbm = pl.BlockSpec(memory_space=pltpu.HBM)
    bf16, f32, dma = jnp.bfloat16, jnp.float32, pltpu.SemaphoreType.DMA
    return pl.pallas_call(
        kernel,
        out_shape=jax.ShapeDtypeStruct((ROWS, W), f32),
        in_specs=[hbm] * 6,
        out_specs=pl.BlockSpec(memory_space=pltpu.VMEM),
        scratch_shapes=[
            pltpu.VMEM((W // 2, 2 * W), bf16),
            pltpu.VMEM((2 * W, W // 2), bf16),
            pltpu.VMEM((2, ROOMS, 8, SUB, 128), bf16),
            pltpu.VMEM((NONE + 1, 3, 8, 128), f32),
            pltpu.VMEM((128, 128), f32),
            pltpu.VMEM((ROWS, W), bf16),
            pltpu.VMEM((PAIRS, 2, ROWS, W), bf16),
            pltpu.VMEM((32 * SUB, 128), f32),
            pltpu.VMEM((SPAN * SUB, 128), f32),
            pltpu.VMEM((PAIRS, 2, 2, 8, 128), f32),
            pltpu.VMEM((64 * SUB, 128), f32),
            pltpu.VMEM((8, ROWS, W), bf16),
            pltpu.VMEM((CHIPS, ROWS, W), bf16),
            pltpu.VMEM((8, 128), jnp.int32),
            pltpu.VMEM((8, 128), f32),
            pltpu.SMEM((8, 128), jnp.int32),
            pltpu.SMEM((8, 128), f32),
            pltpu.SMEM((ROOMS,), jnp.int32),
            pltpu.SMEM((ROOMS,), jnp.int32),
            dma((4,)),
            dma((2,)),
            dma,
            dma,
            dma,
            dma((CHIPS, 2)),
            dma((PAIRS, 2)),
            dma((8,)),
            dma((CHIPS,)),
        ],
        compiler_params=pltpu.CompilerParams(
            collective_id=0, has_side_effects=True, vmem_limit_bytes=48 * 1024 * 1024
        ),
    )(
        *[
            pltpu.with_memory_space_constraint(x, pltpu.HBM)
            for x in (samples, ir, clip_lengths, room_ids, forward_part(W), inverse_part(W))
        ]
    )


def solution(mesh):
    in_specs = (P(("tile", "ir"), None), P(None, "ir", None, None), P(), P())
    out_specs = P(("tile", "ir"), None)
    return jax.shard_map(
        on_device, mesh=mesh, in_specs=in_specs, out_specs=out_specs, check_vma=False
    )
```
